32 devices in a mesh: atom: 8 (over z, x), aux: 4 (over y, core).
Axes of the slice: x: 2, y: 2, z: 4, core: 2. Of those that a mesh axis runs over, the one named last changes fastest.
Arguments:
- three_index: bfloat16 [128, 32, 128, 128], P('atom', 'aux'), may hold values from -6 to 6
- pair_mask: int32 [128, 8, 8], P('atom'), may hold values 0 or 1
- pair_owner: int32 [128, 1], P('atom'), may hold values from 0 to 7; in each aligned block of 16 rows (0 to 15, 16 to 31, ...) at most 2 rows name the same one
- pair_sub: int32 [128], P('atom'), may hold values from 0 to 3
- pair_nu: int32 [128], P('atom'), may hold values from 0 to 31
- live_count: int32 [8], P('atom'), may hold values from 1 to 16, 96 in all
- coefficients: bfloat16 [4096, 128], P('atom'), may hold values from -0.5 to 0.5
- fit_matrix: bfloat16 [32, 32], P('aux'), as said below
Outputs:
- exchange: float32 [4096, 4096], P('atom', 'aux')
The draws below stay inside these ranges and needn't reach their ends.
Inputs may be any that keep to these rules, and one draw needn't show every extreme that they name: `pair_owner`: among the 16 slots of one atom index, at most 2 name the same owner, and in every draw some owner is named exactly 2 times by some atom index's slots. The first live_count[a] slots of atom index a are live; some atom index has all 16 slots live. `fit_matrix`: Symmetric.
All inputs are finite; a program needn't handle non-finite values. No bound on the sum of `pair_mask` or of `live_count` on one device may be relied on, other than what follows from the above.
Results may differ from the reference program's by a relative error of at most 0.012.
Values may be sent and summed in bfloat16 or wider, within the bound.
A program may use at most 128 MiB of HBM per device.

```python
import math
import jax
import jax.numpy as jnp
import numpy as np
from jax import lax

BLK = 128
AB = 8
NOCC = 128
AUX_DEV = 8
MB_DEV = 4
TASK_DEV = 16
CAP = 2
NAUX = 32
NB = 32
NBF = 4096
PAIRS = 128
N_ATOM = 8
N_AUX = 4


def draw_fit_matrix(key, part):
    first_key, second_key = jax.random.split(jax.random.fold_in(key, 17), 2)
    base = jax.random.normal(first_key, (NAUX, NAUX), jnp.float32) * NAUX ** (-0.5)
    matrix = (base + base.T) * 0.7071
    diagonal = jax.random.uniform(second_key, (NAUX,), jnp.float32, -0.5, 0.5)
    matrix = matrix + jnp.diag(diagonal)
    return matrix.astype(jnp.bfloat16)


def with_ends(result, own_key, low, largest):
    longest = result.shape.index(max(result.shape))
    spots = []
    for shift in (0, 1):
        where = [jax.random.randint(jax.random.fold_in(own_key, axis), (), 0, length) for axis, length in enumerate(result.shape)]
        where[longest] = (where[longest] + shift) % result.shape[longest]
        spots.append(tuple(where))
    return result.at[spots[0]].set(low).at[spots[1]].set(largest)


def shard_levels(own_key, shape, cuts, least, largest):
    factor_of, own = 1.0, jax.random.fold_in(own_key, 6)
    for dim, parts in cuts:
        heights = jnp.exp(jax.random.uniform(jax.random.fold_in(own, dim), (parts,), jnp.float32, least / len(cuts), largest / len(cuts)))
        factor_of = factor_of * jnp.repeat(heights, shape[dim] // parts).reshape([-1 if axis == dim else 1 for axis in range(len(shape))])
    return factor_of


def profile(amount, total, limit, lean):
    weights = [(1 << 20) // math.isqrt(rank ** lean) + 1 for rank in range(2, amount + 1)]
    surplus, holding = total - limit - (amount - 1), [1] * (amount - 1)
    while surplus > 0:
        candidates = [i for i in range(amount - 1) if holding[i] < limit]
        mass, remaining = sum([weights[i] for i in candidates]), surplus
        for i in candidates:
            more = min(limit - holding[i], max(1, remaining * weights[i] // mass), surplus)
            holding[i] = holding[i] + more
            surplus = surplus - more
    return np.array([limit] + holding)


def ragged(key, count, total, limit, skew):
    if count == 2:
        one = jax.random.randint(key, (), max(1, total - limit), min(limit, total - 1) + 1)
        return jnp.stack([one, total - one])
    lengths = jnp.asarray(profile(count, total, limit, skew), jnp.int32)
    couples = (count - 1) // 2
    donor, sink = lengths[1:1 + 2 * couples:2], lengths[2:2 + 2 * couples:2]
    slack = jnp.minimum(donor - 1, limit - sink)
    passed = jax.random.randint(jax.random.fold_in(key, 1), (couples,), 0, 1 << 20) % (slack + 1)
    lengths = lengths.at[1:1 + 2 * couples:2].set(donor - passed).at[2:2 + 2 * couples:2].set(sink + passed)
    return lengths[jax.random.permutation(jax.random.fold_in(key, 2), count)]


def shared_out(rng, own, number, rows, amount, top, limit, skew):
    ranking = jax.random.permutation(rng, amount)
    heavy_load, usual = load_shares(amount, rows * top, limit, skew, True), load_shares(amount, rows * top, limit, skew, False)
    places = jnp.arange(amount)

    def named(lengths, turn):
        used = int((lengths > 0).sum())
        fixed = max(1, used // 4)
        moved = fixed + (places - fixed + turn * (used - fixed)) % max(1, amount - fixed)
        return jnp.zeros((amount,), jnp.int32).at[ranking[jnp.where(places < fixed, places, moved)]].set(jnp.asarray(lengths, jnp.int32))

    lengths = jnp.where(number % 4 == 0, named(heavy_load, number // 4), named(usual, number - number // 4 - 1))
    mixed = jax.random.permutation(jax.random.fold_in(own, 3), amount)
    source_of, receiver = mixed[0:amount // 2 * 2:2], mixed[1:amount // 2 * 2:2]
    margin = jnp.minimum(lengths[source_of] - 1, limit - lengths[receiver]) // 2
    margin = jnp.where((source_of == ranking[0]) | (receiver == ranking[0]) | (lengths[receiver] == 0), 0, jnp.maximum(margin, 0))
    moved = jax.random.randint(jax.random.fold_in(own, 4), (amount // 2,), 0, 1 << 20) % (margin + 1)
    lengths = lengths.at[source_of].add(-moved).at[receiver].add(moved)
    labels = jnp.searchsorted(jnp.cumsum(lengths), jnp.arange(rows * top), side="right").astype(jnp.int32)
    listing = labels.reshape(top, rows).T
    listing = listing[jax.random.permutation(jax.random.fold_in(own, 1), rows)]
    turn = jax.random.randint(jax.random.fold_in(own, 2), (rows, 1), 0, top)
    return jnp.take_along_axis(listing, (jnp.arange(top)[None, :] + turn) % top, axis=1)


def load_shares(number_of, total, limit, lean, full):
    loads = [(1 << 20) // math.isqrt(standing ** lean) + 1 for standing in range(1, number_of + 1)]
    largest = limit if full else min(limit, max(-(-total // number_of), total * loads[0] // sum(loads)))
    least = 1 if total - largest >= number_of - 1 else 0
    holding, surplus = [largest] + [least] * (number_of - 1), total - largest - least * (number_of - 1)
    while surplus > 0:
        candidates = [i for i in range(1, number_of) if holding[i] < largest] or [i for i in range(1, number_of) if holding[i] < limit]
        mass, remaining = sum([loads[i] for i in candidates]), surplus
        for i in candidates:
            more = min(limit - holding[i], max(1, remaining * loads[i] // mass), surplus)
            holding[i] = holding[i] + more
            surplus = surplus - more
    return np.array(holding)


def gaussian(stream_key, dims, spread, reach, cuts=(), kind=jnp.bfloat16):
    loudness = shard_levels(stream_key, dims, cuts, -0.22, 0.18) if cuts else 1.0
    drawn = jax.random.normal(stream_key, dims, jnp.float32) * spread * loudness
    return jnp.minimum(jnp.maximum(drawn, -reach), reach).astype(kind)


def setup_inputs(seed: int = 0) -> dict:
    key_of = jax.random.split(jax.random.key(seed), 9)
    three_index = gaussian(key_of[0], (PAIRS, NAUX, BLK, BLK), 1.0, 6.0, ((0, 8), (1, 4)))
    pair_mask = with_ends((jax.random.randint(key_of[1], (PAIRS, AB, AB), 0, 4) < 3).astype(jnp.int32), jax.random.fold_in(key_of[1], 1), 0, 1)
    pair_owner_keys = jax.random.split(jax.random.fold_in(key_of[2], 1), PAIRS // TASK_DEV)
    pair_owner_turns = jax.random.permutation(jax.random.fold_in(key_of[2], 3), PAIRS // TASK_DEV)
    pair_owner = jax.vmap(lambda own, number: shared_out(jax.random.fold_in(key_of[2], 2), own, number, TASK_DEV, N_ATOM, 1, CAP, 2))(pair_owner_keys, pair_owner_turns).reshape((PAIRS, 1))
    pair_sub = with_ends(jax.random.randint(key_of[3], (PAIRS,), 0, MB_DEV), jax.random.fold_in(key_of[3], 1), 0, MB_DEV - 1).astype(jnp.int32)
    pair_nu = with_ends(jax.random.randint(key_of[4], (PAIRS,), 0, NB), jax.random.fold_in(key_of[4], 1), 0, NB - 1).astype(jnp.int32)
    live_count = ragged(key_of[5], N_ATOM, N_ATOM * TASK_DEV * 3 // 4, TASK_DEV, 2).astype(jnp.int32)
    coefficients = gaussian(key_of[6], (NBF, NOCC), BLK ** -0.5, 0.5, ((0, 8),))
    fit_matrix = draw_fit_matrix(jax.random.fold_in(key_of[8], 71), 0)
    return {"three_index": three_index, "pair_mask": pair_mask, "pair_owner": pair_owner, "pair_sub": pair_sub, "pair_nu": pair_nu, "live_count": live_count, "coefficients": coefficients, "fit_matrix": fit_matrix}


def reference(three_index, pair_mask, pair_owner, pair_sub, pair_nu, live_count, coefficients, fit_matrix):
    block_size = three_index.shape[2]
    aux_total = fit_matrix.shape[0]
    basis_total = coefficients.shape[0]
    occupied = coefficients.shape[1]
    shell_size = block_size // pair_mask.shape[1]
    slot_index = jnp.arange(three_index.shape[0], dtype=jnp.int32)
    alive_mask = (slot_index % TASK_DEV) < live_count[slot_index // TASK_DEV]
    mu_blocks = (pair_owner[:, 0] * MB_DEV + pair_sub).astype(jnp.int32)
    zero_index = jnp.zeros((), jnp.int32)

    def add_pair(summed, inputs):
        tile_data, small_mask, nu_block, mu_block, alive_flag = inputs
        expanded = jnp.repeat(jnp.repeat(small_mask, shell_size, 0), shell_size, 1).astype(jnp.float32)
        masked = tile_data.astype(jnp.float32) * expanded
        orbital_rows = lax.dynamic_slice(coefficients, ((nu_block * block_size).astype(jnp.int32), zero_index), (block_size, occupied)).astype(jnp.float32)
        halfway = jnp.einsum("pmn,ni->pmi", masked, orbital_rows)
        rounded = lax.optimization_barrier(halfway.astype(jnp.bfloat16)).astype(jnp.float32)
        rounded = jnp.where(alive_flag, rounded, 0.0)
        start_row = (mu_block * block_size).astype(jnp.int32)
        current = lax.dynamic_slice(summed, (zero_index, start_row, zero_index), (aux_total, block_size, occupied))
        return lax.dynamic_update_slice(summed, current + rounded, (zero_index, start_row, zero_index)), None

    summed, _ = lax.scan(add_pair, jnp.zeros((aux_total, basis_total, occupied), jnp.float32), (three_index, pair_mask, pair_nu, mu_blocks, alive_mask))
    half_transformed = summed.astype(jnp.bfloat16)
    flat_input = lax.optimization_barrier(half_transformed).astype(jnp.float32).reshape(aux_total, basis_total * occupied)
    fitted = jnp.dot(fit_matrix.astype(jnp.float32), flat_input).astype(jnp.bfloat16)
    left_all = half_transformed.reshape(N_AUX, AUX_DEV, basis_total, occupied)
    right_all = fitted.reshape(N_AUX, AUX_DEV, basis_total, occupied)

    def add_share(summed_exchange, pieces):
        left_piece, right_piece = pieces
        left_rows = lax.optimization_barrier(left_piece).astype(jnp.float32).transpose(1, 0, 2).reshape(basis_total, AUX_DEV * occupied)
        right_rows = lax.optimization_barrier(right_piece).astype(jnp.float32).transpose(1, 0, 2).reshape(basis_total, AUX_DEV * occupied)
        partial_value = jnp.dot(left_rows, right_rows.T)
        rounded = lax.optimization_barrier(partial_value.astype(jnp.bfloat16)).astype(jnp.float32)
        return summed_exchange + rounded, None

    exchange, _ = lax.scan(add_share, jnp.zeros((basis_total, basis_total), jnp.float32), (left_all, right_all))
    return exchange * (aux_total * occupied) ** -0.5
```

```python
import functools
import math

import jax
import jax.numpy as jnp
from jax import lax
from jax.experimental import pallas as pl
from jax.experimental.pallas import tpu as pltpu
from jax.sharding import PartitionSpec as P

CAP = 2
MESH = pl.DeviceIdType.MESH


def exchange_kernel(
    atoms, auxes, h_ref, fit_ref, out_ref,
    hall, hx, g, epart, cbuf, ybuf,
    local_sem, sx, sz0, sz, rh, sa, ra, sc, rc, sy, ry,
):
    planes, ys = atoms // 2, auxes // 2
    aux_here, rows, occ = h_ref.shape
    me = lax.axis_index("atom")
    ax = lax.axis_index("aux")
    hi, lo = me // 2, me % 2
    y, c = ax // 2, ax % 2
    partner = {"atom": hi * 2 + 1 - lo, "aux": ax}
    peer = {"atom": me, "aux": y * 2 + 1 - c}

    barrier = pltpu.get_barrier_semaphore()

    def greet(device):
        pl.semaphore_signal(barrier, inc=1, device_id=device, device_id_type=MESH)

    greet(partner)
    greet(peer)
    for d in range(1, ys):
        greet({"atom": me, "aux": ((y + d) % ys) * 2 + c})

    @pl.when(hi > 0)
    def _():
        greet({"atom": me - 2, "aux": ax})

    @pl.when(hi < planes - 1)
    def _():
        greet({"atom": me + 2, "aux": ax})

    before = jnp.minimum(hi, 1)
    behind = jnp.minimum(planes - 1 - hi, 1)
    pl.semaphore_wait(barrier, 1 + ys + before + behind)

    def remote(src, dst, send, recv, device):
        return pltpu.make_async_remote_copy(
            src_ref=src, dst_ref=dst, send_sem=send, recv_sem=recv,
            device_id=device, device_id_type=MESH,
        )

    def to_partner(k, atom, src):
        return remote(src, hall.at[atom], sx.at[k], rh.at[atom], partner)

    def along(atom, src, sem, step):
        return remote(src, hall.at[atom], sem, rh.at[atom], {"atom": me + 2 * step, "aux": ax})

    left_ok, right_ok = hi > 0, hi < planes - 1

    @pl.when(left_ok)
    def _():
        along(me, h_ref, sz0.at[0], -1).start()

    @pl.when(right_ok)
    def _():
        along(me, h_ref, sz0.at[1], 1).start()

    to_partner(0, me, h_ref).start()
    for d in range(1, ys):
        remote(h_ref, hx.at[ax], sa.at[d], ra.at[ax], {"atom": me, "aux": ((y + d) % ys) * 2 + c}).start()
    remote(h_ref, hx.at[ax], sa.at[0], ra.at[ax], peer).start()
    own = pltpu.make_async_copy(h_ref, hall.at[me], local_sem.at[0])
    own.start()
    own_aux = pltpu.make_async_copy(h_ref, hx.at[ax], local_sem.at[1])
    own_aux.start()

    def plane_of(k):
        half = (k + 1) // 2
        return hi + half * (1 - 2 * (k % 2))

    def valid(k):
        p = plane_of(k)
        return (p >= 0) & (p < planes) & (k < 2 * planes - 1)

    def forward_ok(k):
        target = hi - (1 - 2 * (k % 2))
        return valid(k) & (target >= 0) & (target < planes)

    def wait_block(atom):
        remote(h_ref, hall.at[atom], sx.at[0], rh.at[atom], partner).wait_recv()

    def relay(k):
        @pl.when(valid(k))
        def _():
            atom = plane_of(k) * 2 + lo
            wait_block(atom)

            @pl.when(forward_ok(k))
            def _():
                along(atom, hall.at[atom], sz.at[k], -(1 - 2 * (k % 2))).start()

            to_partner(k, atom, hall.at[atom]).start()

    relay(1)
    relay(2)

    for d in range(1, ys):
        src = ((y + d) % ys) * 2 + c
        remote(h_ref, hx.at[src], sa.at[0], ra.at[src], peer).wait_recv()
        remote(hx.at[src], hx.at[src], sa.at[ys - 1 + d], ra.at[src], peer).start()
    for d in range(ys):
        src = ((y + d) % ys) * 2 + 1 - c
        remote(h_ref, hx.at[src], sa.at[0], ra.at[src], peer).wait_recv()
    own_aux.wait()
    own.wait()

    piece = 32

    @pl.loop(0, rows // piece)
    def _(j):
        at = pl.ds(pl.multiple_of(j * piece, piece), piece)
        sums = [jnp.zeros((piece, occ), jnp.float32) for _ in range(aux_here)]
        for p in range(aux_here * auxes):
            block = hx[p // aux_here, p % aux_here, at, :].astype(jnp.float32)
            for q in range(aux_here):
                sums[q] = sums[q] + fit_ref[q, p] * block
        for q in range(aux_here):
            g[at, q * occ:(q + 1) * occ] = sums[q].astype(jnp.bfloat16)

    width = 256

    def product(k):
        p = plane_of(k)

        @pl.when(k > 0)
        def _():
            wait_block(p * 2 + 1 - lo)

        @pl.when(k == 0)
        def _():
            wait_block(hi * 2 + 1 - lo)

        for half in range(2):
            @pl.loop(0, rows // width)
            def _(j):
                at = pl.ds(pl.multiple_of(j * width, width), width)
                right = jnp.concatenate(
                    [hall[p * 2 + half, q, at, :] for q in range(aux_here)], axis=-1
                )
                part = lax.dot_general(
                    g[...], right, (((1,), (1,)), ((), ())), preferred_element_type=jnp.float32
                )
                col = pl.ds(pl.multiple_of(half * rows + j * width, width), width)
                epart[p, :, col] = part.astype(jnp.bfloat16)

        @pl.when(p % 2 != c)
        def _():
            remote(epart.at[p], cbuf.at[p // 2], sc.at[p // 2], rc.at[p // 2], peer).start()

    def join(k):
        p = plane_of(k)
        yt = p // 2

        @pl.when(p % 2 == c)
        def _():
            remote(epart.at[p], cbuf.at[yt], sc.at[yt], rc.at[yt], peer).wait_recv()

            @pl.when(yt != y)
            def _():
                @pl.loop(0, rows // 64)
                def _(j):
                    at = pl.ds(pl.multiple_of(j * 64, 64), 64)
                    total = epart[p, at, :].astype(jnp.float32) + cbuf[yt, at, :].astype(jnp.float32)
                    epart[p, at, :] = total.astype(jnp.bfloat16)

                remote(epart.at[p], ybuf.at[y], sy.at[yt], ry.at[y], {"atom": me, "aux": p}).start()

    @pl.loop(0, 2 * planes)
    def _(k):
        @pl.when(valid(k))
        def _():
            product(k)

        @pl.when(k > 0)
        def _():
            @pl.when(valid(k - 1))
            def _():
                join(k - 1)

        relay(k + 3)

    for d in range(1, ys):
        src = (y + d) % ys
        remote(epart.at[ax], ybuf.at[src], sy.at[src], ry.at[src], peer).wait_recv()

    @pl.loop(0, rows // 64)
    def _(j):
        at = pl.ds(pl.multiple_of(j * 64, 64), 64)
        total = epart[ax, at, :].astype(jnp.float32) + cbuf[y, at, :].astype(jnp.float32)
        for d in range(1, ys):
            total = total + ybuf[(y + d) % ys, at, :].astype(jnp.float32)
        out_ref[at, :] = total

    @pl.when(left_ok)
    def _():
        along(me, h_ref, sz0.at[0], -1).wait_send()

    @pl.when(right_ok)
    def _():
        along(me, h_ref, sz0.at[1], 1).wait_send()

    for k in range(2 * planes - 1):
        @pl.when(valid(k))
        def _():
            to_partner(k, me, h_ref).wait_send()

            if k > 0:
                @pl.when(forward_ok(k))
                def _():
                    along(me, h_ref, sz.at[k], -(1 - 2 * (k % 2))).wait_send()

    for d in range(2 * ys - 1):
        remote(h_ref, hx.at[ax], sa.at[d], ra.at[ax], peer).wait_send()
    for t in range(ys):
        remote(epart.at[ax], cbuf.at[t], sc.at[t], rc.at[t], peer).wait_send()
    for d in range(1, ys):
        remote(epart.at[ax], ybuf.at[y], sy.at[(y + d) % ys], ry.at[y], peer).wait_send()


def exchange_call(h, fit_rows):
    aux_here, rows, occ = h.shape
    atoms, auxes = lax.axis_size("atom"), lax.axis_size("aux")
    planes, ys = atoms // 2, auxes // 2
    columns = rows * atoms // auxes
    dma = pltpu.SemaphoreType.DMA
    return pl.pallas_call(
        functools.partial(exchange_kernel, atoms, auxes),
        out_shape=jax.ShapeDtypeStruct((rows, columns), jnp.float32),
        in_specs=[
            pl.BlockSpec(memory_space=pltpu.VMEM),
            pl.BlockSpec(memory_space=pltpu.SMEM),
        ],
        out_specs=pl.BlockSpec(memory_space=pltpu.VMEM),
        scratch_shapes=[
            pltpu.VMEM((atoms, aux_here, rows, occ), jnp.bfloat16),
            pltpu.VMEM((auxes, aux_here, rows, occ), jnp.bfloat16),
            pltpu.VMEM((rows, aux_here * occ), jnp.bfloat16),
            pltpu.VMEM((auxes, rows, columns), jnp.bfloat16),
            pltpu.VMEM((ys, rows, columns), jnp.bfloat16),
            pltpu.VMEM((ys, rows, columns), jnp.bfloat16),
            dma((2,)),
            dma((2 * planes - 1,)),
            dma((2,)),
            dma((2 * planes - 1,)),
            dma((atoms,)),
            dma((2 * ys - 1,)),
            dma((auxes,)),
            dma((ys,)),
            dma((ys,)),
            dma((ys,)),
            dma((ys,)),
        ],
        compiler_params=pltpu.CompilerParams(
            collective_id=0, has_side_effects=True, vmem_limit_bytes=60 * 1024 * 1024
        ),
    )(h, fit_rows)


def route_kernel(
    atoms, order_ref, nu_ref, three_ref, mask_ref, code_ref, own_ref, out_ref,
    orbitals, outgoing, arrived, codes, acc, summed, landed,
    local_sem, sx, sz0, sz, rh, sd, rd, sk, rk, cross_sem,
):
    planes, middle = atoms // 2, atoms // 2
    cap = code_ref.shape[1]
    per, size, occ = own_ref.shape
    aux_here = three_ref.shape[1]
    share = aux_here // 2
    me = lax.axis_index("atom")
    ax = lax.axis_index("aux")
    hi, lo = me // 2, me % 2
    side, pos = me // middle, me % middle

    def at_atom(atom):
        return {"atom": atom, "aux": ax}

    barrier = pltpu.get_barrier_semaphore()
    for d in range(1, atoms):
        pl.semaphore_signal(
            barrier, inc=1, device_id=at_atom((me + d) % atoms), device_id_type=MESH
        )
    pl.semaphore_wait(barrier, atoms - 1)

    def remote(src, dst, send, recv, device):
        return pltpu.make_async_remote_copy(
            src_ref=src, dst_ref=dst, send_sem=send, recv_sem=recv,
            device_id=device, device_id_type=MESH,
        )

    def spot(atom):
        return orbitals.at[pl.ds(atom * per, per)]

    def to_partner(k, atom, src):
        return remote(src, spot(atom), sx.at[k], rh.at[atom], at_atom(hi * 2 + 1 - lo))

    def along(atom, src, sem, step):
        return remote(src, spot(atom), sem, rh.at[atom], at_atom(me + 2 * step))

    left_ok, right_ok = hi > 0, hi < planes - 1

    @pl.when(left_ok)
    def _():
        along(me, own_ref, sz0.at[0], -1).start()

    @pl.when(right_ok)
    def _():
        along(me, own_ref, sz0.at[1], 1).start()

    to_partner(0, me, own_ref).start()
    own = pltpu.make_async_copy(own_ref, spot(me), local_sem.at[0])
    own.start()

    def plane_of(k):
        half = (k + 1) // 2
        return hi + half * (1 - 2 * (k % 2))

    def valid(k):
        p = plane_of(k)
        return (p >= 0) & (p < planes)

    def forward_ok(k):
        target = hi - (1 - 2 * (k % 2))
        return valid(k) & (target >= 0) & (target < planes)

    def wait_block(atom):
        remote(own_ref, spot(atom), sx.at[0], rh.at[atom], at_atom(hi * 2 + 1 - lo)).wait_recv()

    @pl.loop(1, 2 * planes - 1)
    def _(k):
        @pl.when(valid(k))
        def _():
            atom = plane_of(k) * 2 + lo
            wait_block(atom)

            @pl.when(forward_ok(k))
            def _():
                along(atom, spot(atom), sz.at[k], -(1 - 2 * (k % 2))).start()

            to_partner(k, atom, spot(atom)).start()

    @pl.loop(0, planes)
    def _(p):
        wait_block(p * 2 + 1 - lo)

    own.wait()

    def half_block(place, part):
        slot, nu = order_ref[place], nu_ref[place]
        right = orbitals[nu]
        left = three_ref[slot, part * share:(part + 1) * share] * mask_ref[slot][None, :, :]
        value = jnp.dot(
            left.reshape(share * size, size), right, preferred_element_type=jnp.float32
        )
        return value.reshape(share, size, occ).astype(jnp.bfloat16)

    def target_of(j):
        return (pos + j % (middle - 1) + 1) % middle

    def block(part, j, lane, device):
        return remote(
            outgoing.at[part, j], arrived.at[part, lane], sd.at[part, j], rd.at[part, lane], device
        )

    def start_sends(first, owner_side, part):
        @pl.loop(first, first + middle - 1)
        def _(j):
            q = target_of(j)
            owner = owner_side * middle + q
            lane = (first // (middle - 1)) * middle + pos

            @pl.loop(0, cap)
            def _(r):
                outgoing[part, j, r] = half_block(owner * cap + r, part)

            device = at_atom(side * middle + q)
            if part == 0:
                remote(code_ref.at[owner], codes.at[lane], sk.at[j], rk.at[lane], device).start()
            block(part, j, lane, device).start()

    def fill_own(lane, owner, sem):
        @pl.loop(0, cap)
        def _(r):
            for part in range(2):
                arrived[part, lane, r] = half_block(owner * cap + r, part)

        keep = pltpu.make_async_copy(code_ref.at[owner], codes.at[lane], sem)
        keep.start()
        keep.wait()

    start_sends(0, 1 - side, 0)
    start_sends(0, 1 - side, 1)
    fill_own(pos, (1 - side) * middle + pos, local_sem.at[1])
    start_sends(middle - 1, side, 0)
    start_sends(middle - 1, side, 1)
    fill_own(middle + pos, me, local_sem.at[2])

    def take(src, part):
        hits = [
            [codes[src, r, b] for r in range(cap)]
            for b in range(per)
        ]

        @pl.loop(0, share * (size // 64))
        def _(n):
            p, row = n // (size // 64), n % (size // 64)
            at = pl.ds(pl.multiple_of(row * 64, 64), 64)
            values = [
                arrived[part, src, r, p, at, :].astype(jnp.float32).reshape(8, 8, occ)
                for r in range(cap)
            ]
            for b in range(per):
                to = pl.ds(pl.multiple_of(b * size + row * 64, 64), 64)
                total = acc[part * share + p, to, :].reshape(8, 8, occ)
                for r in range(cap):
                    total = total + values[r] * hits[b][r][None]
                acc[part * share + p, to, :] = total.reshape(64, occ)

    def take_all(base, part):
        span = pl.ds(part * share, share)
        acc[span] = jnp.zeros((share,) + acc.shape[1:], jnp.float32)
        take(base + pos, part)

        @pl.loop(1, middle)
        def _(i):
            src = (pos + middle - i) % middle
            lane = base + src
            device = at_atom(side * middle + src)
            if part == 0:
                remote(code_ref.at[0], codes.at[lane], sk.at[0], rk.at[lane], device).wait_recv()
            block(part, 0, lane, device).wait_recv()
            take(lane, part)

    across = at_atom((1 - side) * middle + pos)
    crossings = []
    for part in range(2):
        take_all(0, part)
        span = pl.ds(part * share, share)
        summed[span] = acc[span].astype(jnp.bfloat16)
        cross = remote(
            summed.at[span], landed.at[span], cross_sem.at[part], cross_sem.at[2 + part], across
        )
        cross.start()
        crossings.append(cross)
    take_all(middle, 0)
    take_all(middle, 1)
    for part in range(2):
        crossings[part].wait_recv()
        span = pl.ds(part * share, share)
        out_ref[span] = (acc[span] + landed[span].astype(jnp.float32)).astype(jnp.bfloat16)
    for cross in crossings:
        cross.wait_send()

    @pl.when(left_ok)
    def _():
        along(me, own_ref, sz0.at[0], -1).wait_send()

    @pl.when(right_ok)
    def _():
        along(me, own_ref, sz0.at[1], 1).wait_send()

    to_partner(0, me, own_ref).wait_send()

    @pl.loop(1, 2 * planes - 1)
    def _(k):
        @pl.when(valid(k))
        def _():
            to_partner(k, me, own_ref).wait_send()

            @pl.when(forward_ok(k))
            def _():
                along(me, own_ref, sz.at[k], -(1 - 2 * (k % 2))).wait_send()

    @pl.loop(0, 2 * middle - 2)
    def _(j):
        device = at_atom(side * middle + target_of(j))
        block(0, j, 0, device).wait_send()
        block(1, j, 0, device).wait_send()
        remote(code_ref.at[0], codes.at[0], sk.at[j], rk.at[0], device).wait_send()


def route_call(order, nu, three_index, mask, codes, coefficients):
    aux_here, size = three_index.shape[1], three_index.shape[2]
    rows, occ = coefficients.shape
    per = rows // size
    atoms = lax.axis_size("atom")
    planes = atoms // 2
    dma = pltpu.SemaphoreType.DMA
    smem = pl.BlockSpec(memory_space=pltpu.SMEM)
    vmem = pl.BlockSpec(memory_space=pltpu.VMEM)
    return pl.pallas_call(
        functools.partial(route_kernel, atoms),
        out_shape=jax.ShapeDtypeStruct((aux_here, rows, occ), jnp.bfloat16),
        in_specs=[smem, smem, vmem, vmem, vmem, vmem],
        out_specs=vmem,
        scratch_shapes=[
            pltpu.VMEM((atoms * per, size, occ), jnp.bfloat16),
            pltpu.VMEM((2, atoms - 2, CAP, aux_here // 2, size, occ), jnp.bfloat16),
            pltpu.VMEM((2, atoms, CAP, aux_here // 2, size, occ), jnp.bfloat16),
            pltpu.VMEM((atoms, CAP, per, 8, 128), jnp.float32),
            pltpu.VMEM((aux_here, rows, occ), jnp.float32),
            pltpu.VMEM((aux_here, rows, occ), jnp.bfloat16),
            pltpu.VMEM((aux_here, rows, occ), jnp.bfloat16),
            dma((3,)),
            dma((2 * planes - 1,)),
            dma((2,)),
            dma((2 * planes - 1,)),
            dma((atoms,)),
            dma((2, atoms - 2)),
            dma((2, atoms)),
            dma((atoms - 2,)),
            dma((atoms,)),
            dma((4,)),
        ],
        compiler_params=pltpu.CompilerParams(
            collective_id=1, has_side_effects=True, vmem_limit_bytes=60 * 1024 * 1024
        ),
    )(order, nu, three_index, mask, codes, coefficients.reshape(per, size, occ))


def fused_kernel(
    planes, auxes, step,
    owner_ref, sub_ref, nu_ref, live_ref, three_hbm, mask_ref, coef_ref, kron_ref, out_ref,
    three, mexp, mrows, orb, order, nus, hits, hits_in, keep, xs, xr, up, dn, zb, own_rows, rows_all, fitted, kron, cs, cr,
    local_sem, orb_recv, orb_own, orb_line, orb_x, orb_core, code_sem, kron_send, kron_recv,
    x_send, x_recv, up_send, up_recv, dn_send, dn_recv,
    own_sem, line_up, line_dn, line_recv, b_send, b_recv, a_send, a_recv, c_send, c_recv,
):
    slot_count, aux_here, size, _ = three_hbm.shape
    per = coef_ref.shape[0]
    rows, occ = per * size, coef_ref.shape[2]
    atoms = planes * 2
    half = per // 2
    chunks = aux_here // step
    shells = mask_ref.shape[1]
    shell = size // shells
    me = lax.axis_index("atom")
    ax = lax.axis_index("aux")
    z, x = me // 2, me % 2
    y, c = ax // 2, ax % 2
    ys = auxes // 2
    above, below = {"atom": me + 2, "aux": ax}, {"atom": me - 2, "aux": ax}
    partner = {"atom": z * 2 + 1 - x, "aux": ax}
    core = {"atom": me, "aux": y * 2 + 1 - c}
    has_up, has_dn = z < planes - 1, z > 0

    def at_aux(u):
        return {"atom": me, "aux": u}

    barrier = pltpu.get_barrier_semaphore()

    def greet(device):
        pl.semaphore_signal(barrier, inc=1, device_id=device, device_id_type=MESH)

    greet(partner)
    for d in range(1, auxes):
        greet(at_aux((ax + d) % auxes))

    @pl.when(has_up)
    def _():
        greet(above)

    @pl.when(has_dn)
    def _():
        greet(below)

    load_three = pltpu.make_async_copy(three_hbm, three, local_sem.at[0])
    load_three.start()
    load_kron = pltpu.make_async_copy(
        kron_ref, kron.at[pl.ds(pl.multiple_of(ax * kron_ref.shape[0], kron_ref.shape[0]), kron_ref.shape[0])], local_sem.at[1]
    )
    load_kron.start()
    load_orb = pltpu.make_async_copy(coef_ref, orb.at[pl.ds(me * per, per)], local_sem.at[2])
    load_orb.start()

    pl.semaphore_wait(
        barrier, auxes + jnp.minimum(z, 1) + jnp.minimum(planes - 1 - z, 1)
    )

    def remote(src, dst, send, recv, device):
        return pltpu.make_async_remote_copy(
            src_ref=src, dst_ref=dst, send_sem=send, recv_sem=recv,
            device_id=device, device_id_type=MESH,
        )

    def spot(atom, part):
        return orb.at[pl.ds(atom * per + part * half, half)]

    own_part = coef_ref.at[pl.ds(c * half, half)]

    def orb_copy(src, atom, part, send, device):
        return remote(src, spot(atom, part), send, orb_recv.at[atom * 2 + part], device)

    @pl.when(has_up)
    def _():
        orb_copy(own_part, me, c, orb_own.at[0], above).start()

    @pl.when(has_dn)
    def _():
        orb_copy(own_part, me, c, orb_own.at[1], below).start()

    orb_copy(own_part, me, c, orb_own.at[2], partner).start()

    def wait_orb(atom, part):
        orb_copy(own_part, atom, part, orb_own.at[0], partner).wait_recv()

    lane_row = lax.broadcasted_iota(jnp.int32, (8, 128), 0)
    live = live_ref[0]

    @pl.loop(0, atoms)
    def _(o):
        def scan(s, carry):
            count, slots, nu, codes = carry
            hit = owner_ref[s] == o
            code = jnp.where(s < live, sub_ref[s] + 1, 0)
            new = []
            for r in range(CAP):
                take = hit & (count == r)
                new.append((
                    jnp.where(take, s, slots[r]),
                    jnp.where(take, nu_ref[s], nu[r]),
                    jnp.where(take, code, codes[r]),
                ))
            count = count + jnp.where(hit, 1, 0)
            return count, tuple(v[0] for v in new), tuple(v[1] for v in new), tuple(v[2] for v in new)

        zero = jnp.int32(0)
        zeros = (zero,) * CAP
        _, slots, nu, codes = lax.fori_loop(0, slot_count, scan, (zero, zeros, zeros, zeros))
        for r in range(CAP):
            index = ((o % 2) * planes + o // 2) * CAP + r
            order[index] = slots[r]
            nus[index] = nu[r]
            hits[index] = jnp.where(lane_row == codes[r] - 1, 1.0, 0.0)

    code_count = planes * CAP
    send_codes = remote(
        hits.at[pl.ds((1 - x) * code_count, code_count)], hits_in, code_sem.at[0], code_sem.at[1], partner
    )
    send_codes.start()

    spread = jnp.where(
        lax.broadcasted_iota(jnp.int32, (shells, size), 1) // shell
        == lax.broadcasted_iota(jnp.int32, (shells, size), 0), 1.0, 0.0
    )
    mrows[...] = jnp.dot(
        mask_ref[...].astype(jnp.float32), spread, preferred_element_type=jnp.float32
    )

    @pl.loop(0, slot_count)
    def _(s):
        small = mrows[pl.ds(pl.multiple_of(s * shells, shells), shells), :]
        for j in range(shells):
            mexp[s, j * shell:(j + 1) * shell, :] = jnp.broadcast_to(
                small[j:j + 1, :], (shell, size)
            ).astype(jnp.bfloat16)

    def pass_orb(p, upward):
        atom = p * 2 + x
        wait_orb(atom, c)
        if upward:
            @pl.when(has_up)
            def _():
                orb_copy(spot(atom, c), atom, c, orb_line.at[p], above).start()
        else:
            @pl.when(has_dn)
            def _():
                orb_copy(spot(atom, c), atom, c, orb_line.at[p], below).start()
        orb_copy(spot(atom, c), atom, c, orb_x.at[p], partner).start()
        orb_copy(spot(atom, c), atom, c, orb_core.at[atom], core).start()

    def hand_orb(p):
        atom = p * 2 + 1 - x
        wait_orb(atom, c)
        orb_copy(spot(atom, c), atom, c, orb_core.at[atom], core).start()

    @pl.loop(1, planes)
    def _(d):
        @pl.when(z - d >= 0)
        def _():
            pass_orb(z - d, True)

        @pl.when(z + d < planes)
        def _():
            pass_orb(z + d, False)

    hand_orb(z)

    @pl.loop(1, planes)
    def _(d):
        @pl.when(z - d >= 0)
        def _():
            hand_orb(z - d)

        @pl.when(z + d < planes)
        def _():
            hand_orb(z + d)

    load_kron.wait()
    load_orb.wait()

    def kron_part(u):
        return kron.at[pl.ds(pl.multiple_of(u * kron_ref.shape[0], kron_ref.shape[0]), kron_ref.shape[0])]

    for d in range(1, auxes):
        remote(kron_ref, kron_part(ax), kron_send.at[d], kron_recv.at[ax], at_aux((ax + d) % auxes)).start()

    @pl.loop(0, planes)
    def _(p):
        wait_orb(p * 2 + 1 - x, 1 - c)

        @pl.when(p != z)
        def _():
            wait_orb(p * 2 + x, 1 - c)

    load_three.wait()
    send_codes.wait_recv()

    def half_block(index, k):
        slot, nu = order[index], nus[index]
        left = three[slot, pl.ds(k * step, step)] * mexp[slot][None, :, :]
        value = jnp.dot(
            left.reshape(step * size, size), orb[nu], preferred_element_type=jnp.float32
        )
        return value.reshape(step, size, occ).astype(jnp.bfloat16)

    def span(k):
        return pl.ds(k * step, step)

    def x_copy(k):
        return remote(xs.at[k], xr.at[k], x_send.at[k], x_recv.at[k], partner)

    def add_dense(p, k, extras, target):
        own_hits = [
            [jnp.broadcast_to(hits[(x * planes + p) * CAP + r, b:b + 1, :], (8, 128))[None] for r in range(CAP)]
            for b in range(per)
        ]
        in_hits = [
            [jnp.broadcast_to(hits_in[p * CAP + r, b:b + 1, :], (8, 128))[None] for r in range(CAP)]
            for b in range(per)
        ]
        strip = 64

        def strips(j, place, row):
            at = pl.ds(pl.multiple_of(row * strip, strip), strip)
            shape = (strip // 8, 8, occ)
            own = [keep[k, p, r, j, at, :].astype(jnp.float32).reshape(shape) for r in range(CAP)]
            other = [xr[k, p, r, j, at, :].astype(jnp.float32).reshape(shape) for r in range(CAP)]
            for b in range(per):
                to = pl.ds(pl.multiple_of(b * size + row * strip, strip), strip)
                total = own[0] * own_hits[b][0] + other[0] * in_hits[b][0]
                for r in range(1, CAP):
                    total = total + own[r] * own_hits[b][r] + other[r] * in_hits[b][r]
                for extra in extras:
                    total = total + extra[p, place, to, :].astype(jnp.float32).reshape(shape)
                value = total.reshape(strip, occ).astype(jnp.bfloat16)
                if target is own_rows:
                    target[place, to, :] = value
                else:
                    target[p, place, to, :] = value

        for j in range(step):
            place = k if step == 1 else k * step + j

            @pl.loop(0, size // strip)
            def _(row):
                strips(j, place, row)

    def up_copy(p, k):
        ref = up.at[p, span(k)]
        return remote(ref, ref, up_send.at[p, k], up_recv.at[p, k], above)

    def dn_copy(p, k):
        ref = dn.at[p, span(k)]
        return remote(ref, ref, dn_send.at[p, k], dn_recv.at[p, k], below)

    def lane_of(p):
        return (p + 2 * planes - ax - 1) % planes

    def b_lane(sender, target):
        return planes - 1 + (sender + auxes - target) % auxes

    def line_copy(src, p, k, send, device):
        return remote(src, zb.at[lane_of(p), span(k)], send, line_recv.at[p, k], device)

    def b_copy(src, p, k):
        return remote(src, zb.at[b_lane(ax, p), span(k)], b_send.at[p, k], b_recv.at[ax, k], at_aux(p))

    def a_piece(column, u, k):
        return rows_all.at[column, u, span(k)]

    def a_copy(column, u, k, which, device):
        ref = a_piece(column, u, k)
        return remote(ref, ref, a_send.at[which, k], a_recv.at[column, u, k], device)

    def own_a_copy(k, which, device):
        return remote(
            own_rows.at[span(k)], a_piece(x, ax, k), a_send.at[which, k], a_recv.at[x, ax, k], device
        )

    def own_copy(k):
        return pltpu.make_async_copy(own_rows.at[span(k)], a_piece(x, ax, k), own_sem.at[k])

    def y_devices():
        return [((y + d) % ys) * 2 + c for d in range(1, ys)]

    def inside(k):
        return (k >= 0) & (k < chunks)

    def reduce_rows(t, zz):
        if zz < planes - 1:
            ku = t - 1 - zz

            @pl.when(inside(ku))
            def _():
                for p in range(planes - 1, zz, -1):
                    if zz > 0:
                        up_copy(p, ku).wait_recv()
                    add_dense(p, ku, [up] if zz > 0 else [], up)
                    up_copy(p, ku).start()

        if zz > 0:
            kd = t - planes + zz

            @pl.when(inside(kd))
            def _():
                for p in range(zz):
                    if zz < planes - 1:
                        dn_copy(p, kd).wait_recv()
                    add_dense(p, kd, [dn] if zz < planes - 1 else [], dn)
                    dn_copy(p, kd).start()

        kh = t - 1 - max(zz, planes - 1 - zz)

        @pl.when(inside(kh))
        def _():
            extras = []
            if zz > 0:
                up_copy(zz, kh).wait_recv()
                extras.append(up)
            if zz < planes - 1:
                dn_copy(zz, kh).wait_recv()
                extras.append(dn)
            add_dense(zz, kh, extras, own_rows)
            mine = own_rows.at[span(kh)]
            own_copy(kh).start()
            if zz < planes - 1:
                line_copy(mine, zz, kh, line_up.at[zz, kh], above).start()
            if zz > 0:
                line_copy(mine, zz, kh, line_dn.at[zz, kh], below).start()
            own_a_copy(kh, 0, partner).start()
            for n, u in enumerate(y_devices()):
                own_a_copy(kh, 7 + 2 * n, at_aux(u)).start()
            own_a_copy(kh, 1, core).start()

    def pass_line(t, zz, p):
        kz = t - 1 - max(p, planes - 1 - p) - abs(zz - p)

        @pl.when(inside(kz))
        def _():
            piece = zb.at[lane_of(p), span(kz)]
            line_copy(piece, p, kz, line_up.at[p, kz], above).wait_recv()
            if p < zz < planes - 1:
                line_copy(piece, p, kz, line_up.at[p, kz], above).start()
            if p > zz > 0:
                line_copy(piece, p, kz, line_dn.at[p, kz], below).start()

            @pl.when(p != ax)
            def _():
                b_copy(piece, p, kz).start()

    def pass_rows(t, zz):
        for d in range(1, planes):
            for p in (zz - d, zz + d):
                if 0 <= p < planes:
                    pass_line(t, zz, p)

        ka = t - 2 - max(zz, planes - 1 - zz)

        @pl.when(inside(ka))
        def _():
            a_copy(1 - x, ax, ka, 0, partner).wait_recv()
            for n, u in enumerate(y_devices()):
                a_copy(1 - x, ax, ka, 8 + 2 * n, at_aux(u)).start()
            a_copy(1 - x, ax, ka, 2, core).start()
            for n, u in enumerate(y_devices()):
                a_copy(x, u, ka, 0, partner).wait_recv()
                a_copy(x, u, ka, 7 + 2 * (ys - 1) + 2 * n, core).start()

        kb = t - 3 - max(zz, planes - 1 - zz)

        @pl.when(inside(kb))
        def _():
            for n, u in enumerate(y_devices()):
                a_copy(1 - x, u, kb, 0, partner).wait_recv()
                a_copy(1 - x, u, kb, 8 + 2 * (ys - 1) + 2 * n, core).start()

    @pl.loop(0, chunks + 2 * planes - 1)
    def _(t):
        @pl.when(t < chunks)
        def _():
            @pl.loop(0, planes)
            def _(p):
                for r in range(CAP):
                    xs[t, p, r] = half_block(((1 - x) * planes + p) * CAP + r, t)

            x_copy(t).start()

            @pl.loop(0, planes)
            def _(p):
                for r in range(CAP):
                    keep[t, p, r] = half_block((x * planes + p) * CAP + r, t)

        @pl.when((t >= 1) & (t <= chunks))
        def _():
            x_copy(t - 1).wait_recv()

        for zz in range(planes):
            @pl.when(z == zz)
            def _():
                reduce_rows(t, zz)
                pass_rows(t, zz)

    for d in range(1, auxes):
        remote(kron_ref, kron_part((ax + d) % auxes), kron_send.at[d], kron_recv.at[(ax + d) % auxes], core).wait_recv()

    @pl.loop(0, chunks)
    def _(k):
        own_copy(k).wait()
        for d in range(ys):
            u = ((y + d) % ys) * 2 + 1 - c
            for column in range(2):
                a_copy(column, u, k, 0, partner).wait_recv()

        @pl.when(z != ax)
        def _():
            for d in range(1, auxes):
                u = (ax + d) % auxes
                remote(
                    zb.at[b_lane(u, ax), span(k)], zb.at[b_lane(u, ax), span(k)],
                    b_send.at[0, k], b_recv.at[u, k], core,
                ).wait_recv()

    total_aux = auxes * aux_here
    strip = kron_ref.shape[0] // aux_here

    def mix(load):
        @pl.loop(0, rows // (2 * strip))
        def _(j):
            spots = [
                pl.ds(pl.multiple_of(j * 2 * strip + h * strip, strip), strip) for h in range(2)
            ]
            right = jnp.concatenate(
                [load(at).reshape(total_aux * strip, occ) for at in spots], axis=-1
            )
            value = jnp.dot(kron[...], right, preferred_element_type=jnp.float32).astype(jnp.bfloat16)
            for h in range(2):
                for q in range(total_aux):
                    fitted[spots[h], q * occ:(q + 1) * occ] = value[
                        q * strip:(q + 1) * strip, h * occ:(h + 1) * occ
                    ]

    @pl.when(z == ax)
    def _():
        mix(lambda at: rows_all[x, :, :, at, :])

    @pl.when(z != ax)
    def _():
        mix(lambda at: jnp.concatenate([zb[b_lane(u, ax), :, at, :] for u in range(auxes)], axis=0))

    block = 256

    def product(column, j):
        at = pl.ds(pl.multiple_of(j * block, block), block)
        left = jnp.concatenate(
            [rows_all[column, q // aux_here, q % aux_here, at, :] for q in range(total_aux)], axis=-1
        )
        return at, lax.dot_general(
            left, fitted[...], (((1,), (1,)), ((), ())), preferred_element_type=jnp.float32
        )

    def c_copy(j):
        at = pl.ds(pl.multiple_of(j * block, block), block)
        return remote(cs.at[at], cr.at[at], c_send.at[j], c_recv.at[j], partner)

    @pl.loop(0, rows // block)
    def _(j):
        at, value = product(1 - x, j)
        cs[at, :] = value.astype(jnp.bfloat16)
        c_copy(j).start()

    @pl.loop(0, rows // block)
    def _(j):
        at, value = product(x, j)
        out_ref[at, pl.ds(pl.multiple_of(x * rows, rows), rows)] = value

    @pl.loop(0, rows // block)
    def _(j):
        c_copy(j).wait_recv()
        at = pl.ds(pl.multiple_of(j * block, block), block)
        out_ref[at, pl.ds(pl.multiple_of((1 - x) * rows, rows), rows)] = cr[at, :].astype(jnp.float32)

    @pl.when(has_up)
    def _():
        orb_copy(own_part, me, c, orb_own.at[0], above).wait_send()

    @pl.when(has_dn)
    def _():
        orb_copy(own_part, me, c, orb_own.at[1], below).wait_send()

    orb_copy(own_part, me, c, orb_own.at[2], partner).wait_send()
    send_codes.wait_send()

    @pl.loop(0, planes)
    def _(p):
        @pl.when(p != z)
        def _():
            @pl.when(((p < z) & has_up) | ((p > z) & has_dn))
            def _():
                orb_copy(own_part, me, c, orb_line.at[p], partner).wait_send()

            orb_copy(own_part, me, c, orb_x.at[p], partner).wait_send()
            orb_copy(own_part, me, c, orb_core.at[p * 2 + x], partner).wait_send()

        orb_copy(own_part, me, c, orb_core.at[p * 2 + 1 - x], partner).wait_send()

    for d in range(1, auxes):
        remote(kron_ref, kron_part(ax), kron_send.at[d], kron_recv.at[ax], core).wait_send()

    @pl.loop(0, chunks)
    def _(k):
        x_copy(k).wait_send()
        for which in range(7 + 4 * (ys - 1)):
            if which < 3 or which >= 7:
                a_copy(x, ax, k, which, partner).wait_send()

        @pl.loop(0, planes)
        def _(p):
            @pl.when(p > z)
            def _():
                up_copy(p, k).wait_send()

            @pl.when(p < z)
            def _():
                dn_copy(p, k).wait_send()

            @pl.when((p <= z) & has_up)
            def _():
                line_copy(a_piece(x, ax, k), z, k, line_up.at[p, k], partner).wait_send()

            @pl.when((p >= z) & has_dn)
            def _():
                line_copy(a_piece(x, ax, k), z, k, line_dn.at[p, k], partner).wait_send()

            @pl.when((p != z) & (p != ax))
            def _():
                b_copy(a_piece(x, ax, k), p, k).wait_send()

    @pl.loop(0, rows // block)
    def _(j):
        c_copy(j).wait_send()


def fused_scratch(planes, auxes, step, slot_count, aux_here, size, occ, per, shells, kron_rows):
    atoms, rows, chunks, ys = planes * 2, per * size, aux_here // step, auxes // 2
    dma = pltpu.SemaphoreType.DMA
    half = jnp.bfloat16
    ways = 7 + 4 * (ys - 1)
    buffers = [
        pltpu.VMEM((slot_count, aux_here, size, size), half),
        pltpu.VMEM((slot_count, size, size), half),
        pltpu.VMEM((slot_count * shells, size), jnp.float32),
        pltpu.VMEM((atoms * per, size, occ), half),
        pltpu.SMEM((atoms * CAP,), jnp.int32),
        pltpu.SMEM((atoms * CAP,), jnp.int32),
        pltpu.VMEM((atoms * CAP, 8, 128), jnp.float32),
        pltpu.VMEM((planes * CAP, 8, 128), jnp.float32),
        pltpu.VMEM((chunks, planes, CAP, step, size, occ), half),
        pltpu.VMEM((chunks, planes, CAP, step, size, occ), half),
        pltpu.VMEM((chunks, planes, CAP, step, size, occ), half),
        pltpu.VMEM((planes, aux_here, rows, occ), half),
        pltpu.VMEM((planes, aux_here, rows, occ), half),
        pltpu.VMEM((planes + auxes - 1, aux_here, rows, occ), half),
        pltpu.VMEM((aux_here, rows, occ), half),
        pltpu.VMEM((2, auxes, aux_here, rows, occ), half),
        pltpu.VMEM((rows, auxes * aux_here * occ), half),
        pltpu.VMEM((auxes * kron_rows, auxes * kron_rows), half),
        pltpu.VMEM((rows, rows), half),
        pltpu.VMEM((rows, rows), half),
    ]
    semaphores = [
        dma((3,)),
        dma((atoms * 2,)),
        dma((3,)),
        dma((planes,)),
        dma((planes,)),
        dma((atoms,)),
        dma((2,)),
        dma((auxes,)),
        dma((auxes,)),
        dma((chunks,)),
        dma((chunks,)),
        dma((planes, chunks)),
        dma((planes, chunks)),
        dma((planes, chunks)),
        dma((planes, chunks)),
        dma((chunks,)),
        dma((planes, chunks)),
        dma((planes, chunks)),
        dma((planes, chunks)),
        dma((planes, chunks)),
        dma((auxes, chunks)),
        dma((ways, chunks)),
        dma((2, auxes, chunks)),
        dma((rows // 256,)),
        dma((rows // 256,)),
    ]
    return buffers, semaphores


VMEM_LIMIT = 60 * 1024 * 1024
STRIP = 16


def fused_plan(planes, auxes, three_index, pair_mask, coefficients):
    slot_count, aux_here, size, _ = three_index.shape
    rows, occ = coefficients.shape
    per, shells = rows // size, pair_mask.shape[1]
    if planes != auxes or per % 2 or per > 8 or rows % 256 or shells % 8:
        return None
    step = 1
    buffers, semaphores = fused_scratch(
        planes, auxes, step, slot_count, aux_here, size, occ, per, shells, aux_here * STRIP
    )
    held = rows * 2 * rows * 4 + 2 * rows * occ * 2
    for ref in buffers:
        held += math.prod(ref.shape) * jnp.dtype(ref.dtype).itemsize
    if held > VMEM_LIMIT - 4 * 1024 * 1024:
        return None
    return step, buffers + semaphores


def fused_call(plan, planes, auxes, three_index, pair_mask, owners, subs, nus, live, coefficients, fit_rows):
    step, scratch = plan
    slot_count, aux_here, size, _ = three_index.shape
    rows, occ = coefficients.shape
    shells = pair_mask.shape[1]
    total_aux = fit_rows.shape[1]
    width = jnp.repeat(jnp.repeat(fit_rows, STRIP, 0), STRIP, 1)
    row = lax.broadcasted_iota(jnp.int32, width.shape, 0) % STRIP
    col = lax.broadcasted_iota(jnp.int32, width.shape, 1) % STRIP
    kron_rows = jnp.where(row == col, width, jnp.zeros_like(width))
    smem = pl.BlockSpec(memory_space=pltpu.SMEM)
    vmem = pl.BlockSpec(memory_space=pltpu.VMEM)
    return pl.pallas_call(
        functools.partial(fused_kernel, planes, auxes, step),
        out_shape=jax.ShapeDtypeStruct((rows, 2 * rows), jnp.float32),
        in_specs=[smem] * 4 + [pl.BlockSpec(memory_space=pl.ANY)] + [vmem] * 3,
        out_specs=vmem,
        scratch_shapes=scratch,
        compiler_params=pltpu.CompilerParams(
            collective_id=2, has_side_effects=True, vmem_limit_bytes=VMEM_LIMIT
        ),
    )(
        owners, subs, nus, live, three_index, pair_mask.reshape(slot_count * shells, shells),
        coefficients.reshape(rows // size, size, occ), kron_rows,
    )


def per_device(
    three_index, pair_mask, pair_owner, pair_sub, pair_nu, live_count, coefficients, fit_matrix
):
    slot_count, aux_here, block_size, _ = three_index.shape
    rows_here, occupied = coefficients.shape
    atom_count = lax.axis_size("atom")
    aux_total = fit_matrix.shape[1]
    planes, auxes = atom_count // 2, lax.axis_size("aux")
    plan = fused_plan(planes, auxes, three_index, pair_mask, coefficients)
    if plan is not None:
        total = fused_call(
            plan, planes, auxes, three_index, pair_mask, pair_owner[:, 0], pair_sub, pair_nu,
            live_count, coefficients, fit_matrix,
        )
        return total * (aux_total * occupied) ** (-0.5)
    shell_size = block_size // pair_mask.shape[1]
    expanded = jnp.repeat(jnp.repeat(pair_mask, shell_size, 1), shell_size, 2).astype(jnp.bfloat16)
    owners = pair_owner[:, 0]
    ahead = jnp.arange(slot_count)[None, :] < jnp.arange(slot_count)[:, None]
    rank_within = jnp.sum(((owners[:, None] == owners[None, :]) & ahead).astype(jnp.int32), 1)
    placement = owners * CAP + rank_within
    routing = (jnp.arange(atom_count * CAP)[:, None] == placement[None, :]).astype(jnp.int32)
    slots = jnp.arange(slot_count, dtype=jnp.int32)

    def placed(values):
        return jnp.sum(routing * values[None, :], 1)

    live_codes = placed(jnp.where(slots < live_count[0], pair_sub + 1, 0))
    blocks = jnp.arange(rows_here // block_size)
    hits = (live_codes[:, None] == blocks[None, :] + 1).astype(jnp.float32)
    hits = hits.reshape(atom_count, CAP, blocks.shape[0], 1, 1)
    local_rows = route_call(
        placed(slots),
        placed(pair_nu),
        three_index,
        expanded,
        jnp.broadcast_to(hits, hits.shape[:3] + (8, 128)),
        coefficients,
    )
    total = exchange_call(local_rows, fit_matrix.astype(jnp.float32))
    return total * (aux_total * occupied) ** (-0.5)


def solution(mesh):
    in_specs = (
        P("atom", "aux", None, None),
        P("atom", None, None),
        P("atom", None),
        P("atom"),
        P("atom"),
        P("atom"),
        P("atom", None),
        P("aux", None),
    )
    out_specs = P("atom", "aux")
    return jax.shard_map(
        per_device, mesh=mesh, in_specs=in_specs, out_specs=out_specs, check_vma=False
    )
```

```python
import functools
import math

import jax
import jax.numpy as jnp
from jax import lax
from jax.experimental import pallas as pl
from jax.experimental.pallas import tpu as pltpu
from jax.sharding import PartitionSpec as P

CAP = 2
MESH = pl.DeviceIdType.MESH


def exchange_kernel(
    atoms, auxes, h_ref, fit_ref, out_ref,
    hall, hx, g, epart, cbuf, ybuf,
    local_sem, sx, sz0, sz, rh, sa, ra, sc, rc, sy, ry,
):
    planes, ys = atoms // 2, auxes // 2
    aux_here, rows, occ = h_ref.shape
    me = lax.axis_index("atom")
    ax = lax.axis_index("aux")
    hi, lo = me // 2, me % 2
    y, c = ax // 2, ax % 2
    partner = {"atom": hi * 2 + 1 - lo, "aux": ax}
    peer = {"atom": me, "aux": y * 2 + 1 - c}

    barrier = pltpu.get_barrier_semaphore()

    def greet(device):
        pl.semaphore_signal(barrier, inc=1, device_id=device, device_id_type=MESH)

    greet(partner)
    greet(peer)
    for d in range(1, ys):
        greet({"atom": me, "aux": ((y + d) % ys) * 2 + c})

    @pl.when(hi > 0)
    def _():
        greet({"atom": me - 2, "aux": ax})

    @pl.when(hi < planes - 1)
    def _():
        greet({"atom": me + 2, "aux": ax})

    before = jnp.minimum(hi, 1)
    behind = jnp.minimum(planes - 1 - hi, 1)
    pl.semaphore_wait(barrier, 1 + ys + before + behind)

    def remote(src, dst, send, recv, device):
        return pltpu.make_async_remote_copy(
            src_ref=src, dst_ref=dst, send_sem=send, recv_sem=recv,
            device_id=device, device_id_type=MESH,
        )

    def to_partner(k, atom, src):
        return remote(src, hall.at[atom], sx.at[k], rh.at[atom], partner)

    def along(atom, src, sem, step):
        return remote(src, hall.at[atom], sem, rh.at[atom], {"atom": me + 2 * step, "aux": ax})

    left_ok, right_ok = hi > 0, hi < planes - 1

    @pl.when(left_ok)
    def _():
        along(me, h_ref, sz0.at[0], -1).start()

    @pl.when(right_ok)
    def _():
        along(me, h_ref, sz0.at[1], 1).start()

    to_partner(0, me, h_ref).start()
    for d in range(1, ys):
        remote(h_ref, hx.at[ax], sa.at[d], ra.at[ax], {"atom": me, "aux": ((y + d) % ys) * 2 + c}).start()
    remote(h_ref, hx.at[ax], sa.at[0], ra.at[ax], peer).start()
    own = pltpu.make_async_copy(h_ref, hall.at[me], local_sem.at[0])
    own.start()
    own_aux = pltpu.make_async_copy(h_ref, hx.at[ax], local_sem.at[1])
    own_aux.start()

    def plane_of(k):
        half = (k + 1) // 2
        return hi + half * (1 - 2 * (k % 2))

    def valid(k):
        p = plane_of(k)
        return (p >= 0) & (p < planes) & (k < 2 * planes - 1)

    def forward_ok(k):
        target = hi - (1 - 2 * (k % 2))
        return valid(k) & (target >= 0) & (target < planes)

    def wait_block(atom):
        remote(h_ref, hall.at[atom], sx.at[0], rh.at[atom], partner).wait_recv()

    def relay(k):
        @pl.when(valid(k))
        def _():
            atom = plane_of(k) * 2 + lo
            wait_block(atom)

            @pl.when(forward_ok(k))
            def _():
                along(atom, hall.at[atom], sz.at[k], -(1 - 2 * (k % 2))).start()

            to_partner(k, atom, hall.at[atom]).start()

    relay(1)
    relay(2)

    for d in range(1, ys):
        src = ((y + d) % ys) * 2 + c
        remote(h_ref, hx.at[src], sa.at[0], ra.at[src], peer).wait_recv()
        remote(hx.at[src], hx.at[src], sa.at[ys - 1 + d], ra.at[src], peer).start()
    for d in range(ys):
        src = ((y + d) % ys) * 2 + 1 - c
        remote(h_ref, hx.at[src], sa.at[0], ra.at[src], peer).wait_recv()
    own_aux.wait()
    own.wait()

    piece = 32

    @pl.loop(0, rows // piece)
    def _(j):
        at = pl.ds(pl.multiple_of(j * piece, piece), piece)
        sums = [jnp.zeros((piece, occ), jnp.float32) for _ in range(aux_here)]
        for p in range(aux_here * auxes):
            block = hx[p // aux_here, p % aux_here, at, :].astype(jnp.float32)
            for q in range(aux_here):
                sums[q] = sums[q] + fit_ref[q, p] * block
        for q in range(aux_here):
            g[at, q * occ:(q + 1) * occ] = sums[q].astype(jnp.bfloat16)

    width = 256

    def product(k):
        p = plane_of(k)

        @pl.when(k > 0)
        def _():
            wait_block(p * 2 + 1 - lo)

        @pl.when(k == 0)
        def _():
            wait_block(hi * 2 + 1 - lo)

        for half in range(2):
            @pl.loop(0, rows // width)
            def _(j):
                at = pl.ds(pl.multiple_of(j * width, width), width)
                right = jnp.concatenate(
                    [hall[p * 2 + half, q, at, :] for q in range(aux_here)], axis=-1
                )
                part = lax.dot_general(
                    g[...], right, (((1,), (1,)), ((), ())), preferred_element_type=jnp.float32
                )
                col = pl.ds(pl.multiple_of(half * rows + j * width, width), width)
                epart[p, :, col] = part.astype(jnp.bfloat16)

        @pl.when(p % 2 != c)
        def _():
            remote(epart.at[p], cbuf.at[p // 2], sc.at[p // 2], rc.at[p // 2], peer).start()

    def join(k):
        p = plane_of(k)
        yt = p // 2

        @pl.when(p % 2 == c)
        def _():
            remote(epart.at[p], cbuf.at[yt], sc.at[yt], rc.at[yt], peer).wait_recv()

            @pl.when(yt != y)
            def _():
                @pl.loop(0, rows // 64)
                def _(j):
                    at = pl.ds(pl.multiple_of(j * 64, 64), 64)
                    total = epart[p, at, :].astype(jnp.float32) + cbuf[yt, at, :].astype(jnp.float32)
                    epart[p, at, :] = total.astype(jnp.bfloat16)

                remote(epart.at[p], ybuf.at[y], sy.at[yt], ry.at[y], {"atom": me, "aux": p}).start()

    @pl.loop(0, 2 * planes)
    def _(k):
        @pl.when(valid(k))
        def _():
            product(k)

        @pl.when(k > 0)
        def _():
            @pl.when(valid(k - 1))
            def _():
                join(k - 1)

        relay(k + 3)

    for d in range(1, ys):
        src = (y + d) % ys
        remote(epart.at[ax], ybuf.at[src], sy.at[src], ry.at[src], peer).wait_recv()

    @pl.loop(0, rows // 64)
    def _(j):
        at = pl.ds(pl.multiple_of(j * 64, 64), 64)
        total = epart[ax, at, :].astype(jnp.float32) + cbuf[y, at, :].astype(jnp.float32)
        for d in range(1, ys):
            total = total + ybuf[(y + d) % ys, at, :].astype(jnp.float32)
        out_ref[at, :] = total

    @pl.when(left_ok)
    def _():
        along(me, h_ref, sz0.at[0], -1).wait_send()

    @pl.when(right_ok)
    def _():
        along(me, h_ref, sz0.at[1], 1).wait_send()

    for k in range(2 * planes - 1):
        @pl.when(valid(k))
        def _():
            to_partner(k, me, h_ref).wait_send()

            if k > 0:
                @pl.when(forward_ok(k))
                def _():
                    along(me, h_ref, sz.at[k], -(1 - 2 * (k % 2))).wait_send()

    for d in range(2 * ys - 1):
        remote(h_ref, hx.at[ax], sa.at[d], ra.at[ax], peer).wait_send()
    for t in range(ys):
        remote(epart.at[ax], cbuf.at[t], sc.at[t], rc.at[t], peer).wait_send()
    for d in range(1, ys):
        remote(epart.at[ax], ybuf.at[y], sy.at[(y + d) % ys], ry.at[y], peer).wait_send()


def exchange_call(h, fit_rows):
    aux_here, rows, occ = h.shape
    atoms, auxes = lax.axis_size("atom"), lax.axis_size("aux")
    planes, ys = atoms // 2, auxes // 2
    columns = rows * atoms // auxes
    dma = pltpu.SemaphoreType.DMA
    return pl.pallas_call(
        functools.partial(exchange_kernel, atoms, auxes),
        out_shape=jax.ShapeDtypeStruct((rows, columns), jnp.float32),
        in_specs=[
            pl.BlockSpec(memory_space=pltpu.VMEM),
            pl.BlockSpec(memory_space=pltpu.SMEM),
        ],
        out_specs=pl.BlockSpec(memory_space=pltpu.VMEM),
        scratch_shapes=[
            pltpu.VMEM((atoms, aux_here, rows, occ), jnp.bfloat16),
            pltpu.VMEM((auxes, aux_here, rows, occ), jnp.bfloat16),
            pltpu.VMEM((rows, aux_here * occ), jnp.bfloat16),
            pltpu.VMEM((auxes, rows, columns), jnp.bfloat16),
            pltpu.VMEM((ys, rows, columns), jnp.bfloat16),
            pltpu.VMEM((ys, rows, columns), jnp.bfloat16),
            dma((2,)),
            dma((2 * planes - 1,)),
            dma((2,)),
            dma((2 * planes - 1,)),
            dma((atoms,)),
            dma((2 * ys - 1,)),
            dma((auxes,)),
            dma((ys,)),
            dma((ys,)),
            dma((ys,)),
            dma((ys,)),
        ],
        compiler_params=pltpu.CompilerParams(
            collective_id=0, has_side_effects=True, vmem_limit_bytes=60 * 1024 * 1024
        ),
    )(h, fit_rows)


def route_kernel(
    atoms, order_ref, nu_ref, three_ref, mask_ref, code_ref, own_ref, out_ref,
    orbitals, outgoing, arrived, codes, acc, summed, landed,
    local_sem, sx, sz0, sz, rh, sd, rd, sk, rk, cross_sem,
):
    planes, middle = atoms // 2, atoms // 2
    cap = code_ref.shape[1]
    per, size, occ = own_ref.shape
    aux_here = three_ref.shape[1]
    share = aux_here // 2
    me = lax.axis_index("atom")
    ax = lax.axis_index("aux")
    hi, lo = me // 2, me % 2
    side, pos = me // middle, me % middle

    def at_atom(atom):
        return {"atom": atom, "aux": ax}

    barrier = pltpu.get_barrier_semaphore()
    for d in range(1, atoms):
        pl.semaphore_signal(
            barrier, inc=1, device_id=at_atom((me + d) % atoms), device_id_type=MESH
        )
    pl.semaphore_wait(barrier, atoms - 1)

    def remote(src, dst, send, recv, device):
        return pltpu.make_async_remote_copy(
            src_ref=src, dst_ref=dst, send_sem=send, recv_sem=recv,
            device_id=device, device_id_type=MESH,
        )

    def spot(atom):
        return orbitals.at[pl.ds(atom * per, per)]

    def to_partner(k, atom, src):
        return remote(src, spot(atom), sx.at[k], rh.at[atom], at_atom(hi * 2 + 1 - lo))

    def along(atom, src, sem, step):
        return remote(src, spot(atom), sem, rh.at[atom], at_atom(me + 2 * step))

    left_ok, right_ok = hi > 0, hi < planes - 1

    @pl.when(left_ok)
    def _():
        along(me, own_ref, sz0.at[0], -1).start()

    @pl.when(right_ok)
    def _():
        along(me, own_ref, sz0.at[1], 1).start()

    to_partner(0, me, own_ref).start()
    own = pltpu.make_async_copy(own_ref, spot(me), local_sem.at[0])
    own.start()

    def plane_of(k):
        half = (k + 1) // 2
        return hi + half * (1 - 2 * (k % 2))

    def valid(k):
        p = plane_of(k)
        return (p >= 0) & (p < planes)

    def forward_ok(k):
        target = hi - (1 - 2 * (k % 2))
        return valid(k) & (target >= 0) & (target < planes)

    def wait_block(atom):
        remote(own_ref, spot(atom), sx.at[0], rh.at[atom], at_atom(hi * 2 + 1 - lo)).wait_recv()

    @pl.loop(1, 2 * planes - 1)
    def _(k):
        @pl.when(valid(k))
        def _():
            atom = plane_of(k) * 2 + lo
            wait_block(atom)

            @pl.when(forward_ok(k))
            def _():
                along(atom, spot(atom), sz.at[k], -(1 - 2 * (k % 2))).start()

            to_partner(k, atom, spot(atom)).start()

    @pl.loop(0, planes)
    def _(p):
        wait_block(p * 2 + 1 - lo)

    own.wait()

    def half_block(place, part):
        slot, nu = order_ref[place], nu_ref[place]
        right = orbitals[nu]
        left = three_ref[slot, part * share:(part + 1) * share] * mask_ref[slot][None, :, :]
        value = jnp.dot(
            left.reshape(share * size, size), right, preferred_element_type=jnp.float32
        )
        return value.reshape(share, size, occ).astype(jnp.bfloat16)

    def target_of(j):
        return (pos + j % (middle - 1) + 1) % middle

    def block(part, j, lane, device):
        return remote(
            outgoing.at[part, j], arrived.at[part, lane], sd.at[part, j], rd.at[part, lane], device
        )

    def start_sends(first, owner_side, part):
        @pl.loop(first, first + middle - 1)
        def _(j):
            q = target_of(j)
            owner = owner_side * middle + q
            lane = (first // (middle - 1)) * middle + pos

            @pl.loop(0, cap)
            def _(r):
                outgoing[part, j, r] = half_block(owner * cap + r, part)

            device = at_atom(side * middle + q)
            if part == 0:
                remote(code_ref.at[owner], codes.at[lane], sk.at[j], rk.at[lane], device).start()
            block(part, j, lane, device).start()

    def fill_own(lane, owner, sem):
        @pl.loop(0, cap)
        def _(r):
            for part in range(2):
                arrived[part, lane, r] = half_block(owner * cap + r, part)

        keep = pltpu.make_async_copy(code_ref.at[owner], codes.at[lane], sem)
        keep.start()
        keep.wait()

    start_sends(0, 1 - side, 0)
    start_sends(0, 1 - side, 1)
    fill_own(pos, (1 - side) * middle + pos, local_sem.at[1])
    start_sends(middle - 1, side, 0)
    start_sends(middle - 1, side, 1)
    fill_own(middle + pos, me, local_sem.at[2])

    def take(src, part):
        hits = [
            [codes[src, r, b] for r in range(cap)]
            for b in range(per)
        ]

        @pl.loop(0, share * (size // 64))
        def _(n):
            p, row = n // (size // 64), n % (size // 64)
            at = pl.ds(pl.multiple_of(row * 64, 64), 64)
            values = [
                arrived[part, src, r, p, at, :].astype(jnp.float32).reshape(8, 8, occ)
                for r in range(cap)
            ]
            for b in range(per):
                to = pl.ds(pl.multiple_of(b * size + row * 64, 64), 64)
                total = acc[part * share + p, to, :].reshape(8, 8, occ)
                for r in range(cap):
                    total = total + values[r] * hits[b][r][None]
                acc[part * share + p, to, :] = total.reshape(64, occ)

    def take_all(base, part):
        span = pl.ds(part * share, share)
        acc[span] = jnp.zeros((share,) + acc.shape[1:], jnp.float32)
        take(base + pos, part)

        @pl.loop(1, middle)
        def _(i):
            src = (pos + middle - i) % middle
            lane = base + src
            device = at_atom(side * middle + src)
            if part == 0:
                remote(code_ref.at[0], codes.at[lane], sk.at[0], rk.at[lane], device).wait_recv()
            block(part, 0, lane, device).wait_recv()
            take(lane, part)

    across = at_atom((1 - side) * middle + pos)
    crossings = []
    for part in range(2):
        take_all(0, part)
        span = pl.ds(part * share, share)
        summed[span] = acc[span].astype(jnp.bfloat16)
        cross = remote(
            summed.at[span], landed.at[span], cross_sem.at[part], cross_sem.at[2 + part], across
        )
        cross.start()
        crossings.append(cross)
    take_all(middle, 0)
    take_all(middle, 1)
    for part in range(2):
        crossings[part].wait_recv()
        span = pl.ds(part * share, share)
        out_ref[span] = (acc[span] + landed[span].astype(jnp.float32)).astype(jnp.bfloat16)
    for cross in crossings:
        cross.wait_send()

    @pl.when(left_ok)
    def _():
        along(me, own_ref, sz0.at[0], -1).wait_send()

    @pl.when(right_ok)
    def _():
        along(me, own_ref, sz0.at[1], 1).wait_send()

    to_partner(0, me, own_ref).wait_send()

    @pl.loop(1, 2 * planes - 1)
    def _(k):
        @pl.when(valid(k))
        def _():
            to_partner(k, me, own_ref).wait_send()

            @pl.when(forward_ok(k))
            def _():
                along(me, own_ref, sz.at[k], -(1 - 2 * (k % 2))).wait_send()

    @pl.loop(0, 2 * middle - 2)
    def _(j):
        device = at_atom(side * middle + target_of(j))
        block(0, j, 0, device).wait_send()
        block(1, j, 0, device).wait_send()
        remote(code_ref.at[0], codes.at[0], sk.at[j], rk.at[0], device).wait_send()


def route_call(order, nu, three_index, mask, codes, coefficients):
    aux_here, size = three_index.shape[1], three_index.shape[2]
    rows, occ = coefficients.shape
    per = rows // size
    atoms = lax.axis_size("atom")
    planes = atoms // 2
    dma = pltpu.SemaphoreType.DMA
    smem = pl.BlockSpec(memory_space=pltpu.SMEM)
    vmem = pl.BlockSpec(memory_space=pltpu.VMEM)
    return pl.pallas_call(
        functools.partial(route_kernel, atoms),
        out_shape=jax.ShapeDtypeStruct((aux_here, rows, occ), jnp.bfloat16),
        in_specs=[smem, smem, vmem, vmem, vmem, vmem],
        out_specs=vmem,
        scratch_shapes=[
            pltpu.VMEM((atoms * per, size, occ), jnp.bfloat16),
            pltpu.VMEM((2, atoms - 2, CAP, aux_here // 2, size, occ), jnp.bfloat16),
            pltpu.VMEM((2, atoms, CAP, aux_here // 2, size, occ), jnp.bfloat16),
            pltpu.VMEM((atoms, CAP, per, 8, 128), jnp.float32),
            pltpu.VMEM((aux_here, rows, occ), jnp.float32),
            pltpu.VMEM((aux_here, rows, occ), jnp.bfloat16),
            pltpu.VMEM((aux_here, rows, occ), jnp.bfloat16),
            dma((3,)),
            dma((2 * planes - 1,)),
            dma((2,)),
            dma((2 * planes - 1,)),
            dma((atoms,)),
            dma((2, atoms - 2)),
            dma((2, atoms)),
            dma((atoms - 2,)),
            dma((atoms,)),
            dma((4,)),
        ],
        compiler_params=pltpu.CompilerParams(
            collective_id=1, has_side_effects=True, vmem_limit_bytes=60 * 1024 * 1024
        ),
    )(order, nu, three_index, mask, codes, coefficients.reshape(per, size, occ))


def fused_kernel(
    planes, auxes, split,
    owner_ref, sub_ref, nu_ref, live_ref, three_hbm, mask_ref, coef_ref, kron_ref, out_ref,
    three, mexp, mrows, orb, order, nus, hits, hits_in, keep, xs, xr, up, dn, zb, own_rows, rows_all, fitted, kron, cs, cr,
    local_sem, orb_recv, orb_own, orb_line, orb_x, orb_core, code_sem, kron_send, kron_recv,
    x_send, x_recv, up_send, up_recv, dn_send, dn_recv,
    own_sem, line_up, line_dn, line_recv, b_send, b_recv, a_send, a_recv, c_send, c_recv,
):
    slot_count, aux_here, size, _ = three_hbm.shape
    per = coef_ref.shape[0]
    rows, occ = per * size, coef_ref.shape[2]
    atoms = planes * 2
    half = per // 2
    chunks, part = aux_here * split, size // split
    group = per * part
    shells = mask_ref.shape[1]
    shell = size // shells
    me = lax.axis_index("atom")
    ax = lax.axis_index("aux")
    z, x = me // 2, me % 2
    y, c = ax // 2, ax % 2
    ys = auxes // 2
    above, below = {"atom": me + 2, "aux": ax}, {"atom": me - 2, "aux": ax}
    partner = {"atom": z * 2 + 1 - x, "aux": ax}
    core = {"atom": me, "aux": y * 2 + 1 - c}
    has_up, has_dn = z < planes - 1, z > 0

    def at_aux(u):
        return {"atom": me, "aux": u}

    barrier = pltpu.get_barrier_semaphore()

    def greet(device):
        pl.semaphore_signal(barrier, inc=1, device_id=device, device_id_type=MESH)

    greet(partner)
    for d in range(1, auxes):
        greet(at_aux((ax + d) % auxes))

    @pl.when(has_up)
    def _():
        greet(above)

    @pl.when(has_dn)
    def _():
        greet(below)

    load_three = pltpu.make_async_copy(three_hbm, three, local_sem.at[0])
    load_three.start()
    load_kron = pltpu.make_async_copy(
        kron_ref, kron.at[pl.ds(pl.multiple_of(ax * kron_ref.shape[0], kron_ref.shape[0]), kron_ref.shape[0])], local_sem.at[1]
    )
    load_kron.start()
    load_orb = pltpu.make_async_copy(coef_ref, orb.at[pl.ds(me * per, per)], local_sem.at[2])
    load_orb.start()

    pl.semaphore_wait(
        barrier, auxes + jnp.minimum(z, 1) + jnp.minimum(planes - 1 - z, 1)
    )

    def remote(src, dst, send, recv, device):
        return pltpu.make_async_remote_copy(
            src_ref=src, dst_ref=dst, send_sem=send, recv_sem=recv,
            device_id=device, device_id_type=MESH,
        )

    def spot(atom, part):
        return orb.at[pl.ds(atom * per + part * half, half)]

    own_part = coef_ref.at[pl.ds(c * half, half)]

    def orb_copy(src, atom, part, send, device):
        return remote(src, spot(atom, part), send, orb_recv.at[atom * 2 + part], device)

    @pl.when(has_up)
    def _():
        orb_copy(own_part, me, c, orb_own.at[0], above).start()

    @pl.when(has_dn)
    def _():
        orb_copy(own_part, me, c, orb_own.at[1], below).start()

    orb_copy(own_part, me, c, orb_own.at[2], partner).start()

    def wait_orb(atom, part):
        orb_copy(own_part, atom, part, orb_own.at[0], partner).wait_recv()

    lane_row = lax.broadcasted_iota(jnp.int32, (8, 128), 0)
    live = live_ref[0]

    @pl.loop(0, atoms)
    def _(o):
        def scan(s, carry):
            count, slots, nu, codes = carry
            hit = owner_ref[s] == o
            code = jnp.where(s < live, sub_ref[s] + 1, 0)
            new = []
            for r in range(CAP):
                take = hit & (count == r)
                new.append((
                    jnp.where(take, s, slots[r]),
                    jnp.where(take, nu_ref[s], nu[r]),
                    jnp.where(take, code, codes[r]),
                ))
            count = count + jnp.where(hit, 1, 0)
            return count, tuple(v[0] for v in new), tuple(v[1] for v in new), tuple(v[2] for v in new)

        zero = jnp.int32(0)
        zeros = (zero,) * CAP
        _, slots, nu, codes = lax.fori_loop(0, slot_count, scan, (zero, zeros, zeros, zeros))
        for r in range(CAP):
            index = ((o % 2) * planes + o // 2) * CAP + r
            order[index] = slots[r]
            nus[index] = nu[r]
            hits[index] = jnp.where(lane_row == codes[r] - 1, 1.0, 0.0)

    code_count = planes * CAP
    send_codes = remote(
        hits.at[pl.ds((1 - x) * code_count, code_count)], hits_in, code_sem.at[0], code_sem.at[1], partner
    )
    send_codes.start()

    spread = jnp.where(
        lax.broadcasted_iota(jnp.int32, (shells, size), 1) // shell
        == lax.broadcasted_iota(jnp.int32, (shells, size), 0), 1.0, 0.0
    )
    mrows[...] = jnp.dot(
        mask_ref[...].astype(jnp.float32), spread, preferred_element_type=jnp.float32
    )

    @pl.loop(0, slot_count)
    def _(s):
        small = mrows[pl.ds(pl.multiple_of(s * shells, shells), shells), :]
        for j in range(shells):
            mexp[s, j * shell:(j + 1) * shell, :] = jnp.broadcast_to(
                small[j:j + 1, :], (shell, size)
            ).astype(jnp.bfloat16)

    def pass_orb(p, upward):
        atom = p * 2 + x
        wait_orb(atom, c)
        if upward:
            @pl.when(has_up)
            def _():
                orb_copy(spot(atom, c), atom, c, orb_line.at[p], above).start()
        else:
            @pl.when(has_dn)
            def _():
                orb_copy(spot(atom, c), atom, c, orb_line.at[p], below).start()
        orb_copy(spot(atom, c), atom, c, orb_x.at[p], partner).start()
        orb_copy(spot(atom, c), atom, c, orb_core.at[atom], core).start()

    def hand_orb(p):
        atom = p * 2 + 1 - x
        wait_orb(atom, c)
        orb_copy(spot(atom, c), atom, c, orb_core.at[atom], core).start()

    @pl.loop(1, planes)
    def _(d):
        @pl.when(z - d >= 0)
        def _():
            pass_orb(z - d, True)

        @pl.when(z + d < planes)
        def _():
            pass_orb(z + d, False)

    hand_orb(z)

    @pl.loop(1, planes)
    def _(d):
        @pl.when(z - d >= 0)
        def _():
            hand_orb(z - d)

        @pl.when(z + d < planes)
        def _():
            hand_orb(z + d)

    load_kron.wait()
    load_orb.wait()

    def kron_part(u):
        return kron.at[pl.ds(pl.multiple_of(u * kron_ref.shape[0], kron_ref.shape[0]), kron_ref.shape[0])]

    for d in range(1, auxes):
        remote(kron_ref, kron_part(ax), kron_send.at[d], kron_recv.at[ax], at_aux((ax + d) % auxes)).start()

    @pl.loop(0, planes)
    def _(p):
        wait_orb(p * 2 + 1 - x, 1 - c)

        @pl.when(p != z)
        def _():
            wait_orb(p * 2 + x, 1 - c)

    load_three.wait()
    send_codes.wait_recv()

    def half_block(index, k):
        slot, nu = order[index], nus[index]
        at = pl.ds(pl.multiple_of((k % split) * part, part), part)
        left = three[slot, k // split, at, :] * mexp[slot, at, :]
        return jnp.dot(left, orb[nu], preferred_element_type=jnp.float32).astype(jnp.bfloat16)

    def x_copy(k):
        return remote(xs.at[k], xr.at[k], x_send.at[k], x_recv.at[k], partner)

    def add_dense(p, k, extras, target):
        own_hits = [
            [jnp.broadcast_to(hits[(x * planes + p) * CAP + r, b:b + 1, :], (8, 128))[None] for r in range(CAP)]
            for b in range(per)
        ]
        in_hits = [
            [jnp.broadcast_to(hits_in[p * CAP + r, b:b + 1, :], (8, 128))[None] for r in range(CAP)]
            for b in range(per)
        ]
        shape = (part // 8, 8, occ)
        own = [keep[k, p, r].astype(jnp.float32).reshape(shape) for r in range(CAP)]
        other = [xr[k, p, r].astype(jnp.float32).reshape(shape) for r in range(CAP)]
        for b in range(per):
            to = slice(b * part, (b + 1) * part)
            total = own[0] * own_hits[b][0] + other[0] * in_hits[b][0]
            for r in range(1, CAP):
                total = total + own[r] * own_hits[b][r] + other[r] * in_hits[b][r]
            for extra in extras:
                total = total + extra[p, k, to, :].astype(jnp.float32).reshape(shape)
            value = total.reshape(part, occ).astype(jnp.bfloat16)
            if target is own_rows:
                target[k, to, :] = value
            else:
                target[p, k, to, :] = value

    def up_copy(p, k):
        ref = up.at[p, k]
        return remote(ref, ref, up_send.at[p, k], up_recv.at[p, k], above)

    def dn_copy(p, k):
        ref = dn.at[p, k]
        return remote(ref, ref, dn_send.at[p, k], dn_recv.at[p, k], below)

    def lane_of(p):
        return (p + 2 * planes - ax - 1) % planes

    def b_lane(sender, target):
        return planes - 1 + (sender + auxes - target) % auxes

    def line_copy(src, p, k, send, device):
        return remote(src, zb.at[lane_of(p), k], send, line_recv.at[p, k], device)

    def b_copy(src, p, k):
        return remote(src, zb.at[b_lane(ax, p), k], b_send.at[p, k], b_recv.at[ax, k], at_aux(p))

    def a_piece(column, u, k):
        return rows_all.at[column, u, k]

    def a_copy(column, u, k, which, device):
        ref = a_piece(column, u, k)
        return remote(ref, ref, a_send.at[which, k], a_recv.at[column, u, k], device)

    def own_a_copy(k, which, device):
        return remote(
            own_rows.at[k], a_piece(x, ax, k), a_send.at[which, k], a_recv.at[x, ax, k], device
        )

    def own_copy(k):
        return pltpu.make_async_copy(own_rows.at[k], a_piece(x, ax, k), own_sem.at[k])

    def y_devices():
        return [((y + d) % ys) * 2 + c for d in range(1, ys)]

    def inside(k):
        return (k >= 0) & (k < chunks)

    def reduce_rows(t, zz):
        if zz < planes - 1:
            ku = t - 1 - zz

            @pl.when(inside(ku))
            def _():
                for p in range(planes - 1, zz, -1):
                    if zz > 0:
                        up_copy(p, ku).wait_recv()
                    add_dense(p, ku, [up] if zz > 0 else [], up)
                    up_copy(p, ku).start()

        if zz > 0:
            kd = t - planes + zz

            @pl.when(inside(kd))
            def _():
                for p in range(zz):
                    if zz < planes - 1:
                        dn_copy(p, kd).wait_recv()
                    add_dense(p, kd, [dn] if zz < planes - 1 else [], dn)
                    dn_copy(p, kd).start()

        kh = t - 1 - max(zz, planes - 1 - zz)

        @pl.when(inside(kh))
        def _():
            extras = []
            if zz > 0:
                up_copy(zz, kh).wait_recv()
                extras.append(up)
            if zz < planes - 1:
                dn_copy(zz, kh).wait_recv()
                extras.append(dn)
            add_dense(zz, kh, extras, own_rows)
            mine = own_rows.at[kh]
            own_copy(kh).start()
            if zz < planes - 1:
                line_copy(mine, zz, kh, line_up.at[zz, kh], above).start()
            if zz > 0:
                line_copy(mine, zz, kh, line_dn.at[zz, kh], below).start()
            own_a_copy(kh, 0, partner).start()
            for n, u in enumerate(y_devices()):
                own_a_copy(kh, 7 + 2 * n, at_aux(u)).start()
            own_a_copy(kh, 1, core).start()

    def pass_line(t, zz, p):
        kz = t - 1 - max(p, planes - 1 - p) - abs(zz - p)

        @pl.when(inside(kz))
        def _():
            piece = zb.at[lane_of(p), kz]
            line_copy(piece, p, kz, line_up.at[p, kz], above).wait_recv()
            if p < zz < planes - 1:
                line_copy(piece, p, kz, line_up.at[p, kz], above).start()
            if p > zz > 0:
                line_copy(piece, p, kz, line_dn.at[p, kz], below).start()

            @pl.when(p != ax)
            def _():
                b_copy(piece, p, kz).start()

    def pass_rows(t, zz):
        for d in range(1, planes):
            for p in (zz - d, zz + d):
                if 0 <= p < planes:
                    pass_line(t, zz, p)

        ka = t - 2 - max(zz, planes - 1 - zz)

        @pl.when(inside(ka))
        def _():
            a_copy(1 - x, ax, ka, 0, partner).wait_recv()
            for n, u in enumerate(y_devices()):
                a_copy(1 - x, ax, ka, 8 + 2 * n, at_aux(u)).start()
            a_copy(1 - x, ax, ka, 2, core).start()
            for n, u in enumerate(y_devices()):
                a_copy(x, u, ka, 0, partner).wait_recv()
                a_copy(x, u, ka, 7 + 2 * (ys - 1) + 2 * n, core).start()

        kb = t - 3 - max(zz, planes - 1 - zz)

        @pl.when(inside(kb))
        def _():
            for n, u in enumerate(y_devices()):
                a_copy(1 - x, u, kb, 0, partner).wait_recv()
                a_copy(1 - x, u, kb, 8 + 2 * (ys - 1) + 2 * n, core).start()

    @pl.loop(0, chunks + 2 * planes - 1)
    def _(t):
        @pl.when(t < chunks)
        def _():
            @pl.loop(0, planes)
            def _(p):
                for r in range(CAP):
                    xs[t, p, r] = half_block(((1 - x) * planes + p) * CAP + r, t)

            x_copy(t).start()

            @pl.loop(0, planes)
            def _(p):
                for r in range(CAP):
                    keep[t, p, r] = half_block((x * planes + p) * CAP + r, t)

        @pl.when((t >= 1) & (t <= chunks))
        def _():
            x_copy(t - 1).wait_recv()

        for zz in range(planes):
            @pl.when(z == zz)
            def _():
                reduce_rows(t, zz)
                pass_rows(t, zz)

    for d in range(1, auxes):
        remote(kron_ref, kron_part((ax + d) % auxes), kron_send.at[d], kron_recv.at[(ax + d) % auxes], core).wait_recv()

    @pl.loop(0, chunks)
    def _(k):
        own_copy(k).wait()
        for d in range(ys):
            u = ((y + d) % ys) * 2 + 1 - c
            for column in range(2):
                a_copy(column, u, k, 0, partner).wait_recv()

        @pl.when(z != ax)
        def _():
            for d in range(1, auxes):
                u = (ax + d) % auxes
                remote(
                    zb.at[b_lane(u, ax), k], zb.at[b_lane(u, ax), k],
                    b_send.at[0, k], b_recv.at[u, k], core,
                ).wait_recv()

    total_aux = auxes * aux_here
    strip = kron_ref.shape[0] // aux_here
    pairs = [(u, p) for u in range(auxes) for p in range(aux_here)]

    def mix(load):
        for h in range(split):
            @pl.loop(0, group // (2 * strip))
            def _(j):
                right = jnp.concatenate([
                    jnp.concatenate([
                        load(u, p * split + h, pl.ds(pl.multiple_of((2 * j + e) * strip, strip), strip))
                        for u, p in pairs
                    ], axis=0)
                    for e in range(2)
                ], axis=-1)
                value = jnp.dot(kron[...], right, preferred_element_type=jnp.float32).astype(jnp.bfloat16)
                for e in range(2):
                    place = (2 * j + e) * strip
                    to = (place // part) * size + h * part + place % part
                    to = pl.ds(pl.multiple_of(to, strip), strip)
                    for q in range(total_aux):
                        fitted[to, q * occ:(q + 1) * occ] = value[
                            q * strip:(q + 1) * strip, e * occ:(e + 1) * occ
                        ]

    @pl.when(z == ax)
    def _():
        mix(lambda u, k, at: rows_all[x, u, k, at, :])

    @pl.when(z != ax)
    def _():
        mix(lambda u, k, at: zb[b_lane(u, ax), k, at, :])

    def product(column, h):
        left = jnp.concatenate([rows_all[column, u, p * split + h] for u, p in pairs], axis=-1)
        return lax.dot_general(
            left, fitted[...], (((1,), (1,)), ((), ())), preferred_element_type=jnp.float32
        )

    def c_copy(h):
        return remote(cs.at[h], cr.at[h], c_send.at[h], c_recv.at[h], partner)

    def place_rows(h, column, value):
        for b in range(per):
            to = pl.ds(pl.multiple_of(b * size + h * part, part), part)
            out_ref[to, pl.ds(pl.multiple_of(column * rows, rows), rows)] = value[b * part:(b + 1) * part, :]

    @pl.loop(0, split)
    def _(h):
        cs[h] = product(1 - x, h).astype(jnp.bfloat16)
        c_copy(h).start()

    @pl.loop(0, split)
    def _(h):
        place_rows(h, x, product(x, h))

    @pl.loop(0, split)
    def _(h):
        c_copy(h).wait_recv()
        place_rows(h, 1 - x, cr[h].astype(jnp.float32))

    @pl.when(has_up)
    def _():
        orb_copy(own_part, me, c, orb_own.at[0], above).wait_send()

    @pl.when(has_dn)
    def _():
        orb_copy(own_part, me, c, orb_own.at[1], below).wait_send()

    orb_copy(own_part, me, c, orb_own.at[2], partner).wait_send()
    send_codes.wait_send()

    @pl.loop(0, planes)
    def _(p):
        @pl.when(p != z)
        def _():
            @pl.when(((p < z) & has_up) | ((p > z) & has_dn))
            def _():
                orb_copy(own_part, me, c, orb_line.at[p], partner).wait_send()

            orb_copy(own_part, me, c, orb_x.at[p], partner).wait_send()
            orb_copy(own_part, me, c, orb_core.at[p * 2 + x], partner).wait_send()

        orb_copy(own_part, me, c, orb_core.at[p * 2 + 1 - x], partner).wait_send()

    for d in range(1, auxes):
        remote(kron_ref, kron_part(ax), kron_send.at[d], kron_recv.at[ax], core).wait_send()

    @pl.loop(0, chunks)
    def _(k):
        x_copy(k).wait_send()
        for which in range(7 + 4 * (ys - 1)):
            if which < 3 or which >= 7:
                a_copy(x, ax, k, which, partner).wait_send()

        @pl.loop(0, planes)
        def _(p):
            @pl.when(p > z)
            def _():
                up_copy(p, k).wait_send()

            @pl.when(p < z)
            def _():
                dn_copy(p, k).wait_send()

            @pl.when((p <= z) & has_up)
            def _():
                line_copy(a_piece(x, ax, k), z, k, line_up.at[p, k], partner).wait_send()

            @pl.when((p >= z) & has_dn)
            def _():
                line_copy(a_piece(x, ax, k), z, k, line_dn.at[p, k], partner).wait_send()

            @pl.when((p != z) & (p != ax))
            def _():
                b_copy(a_piece(x, ax, k), p, k).wait_send()

    @pl.loop(0, split)
    def _(h):
        c_copy(h).wait_send()


def fused_scratch(planes, auxes, split, slot_count, aux_here, size, occ, per, shells, kron_rows):
    atoms, rows, chunks, ys = planes * 2, per * size, aux_here * split, auxes // 2
    part, group = size // split, rows // split
    dma = pltpu.SemaphoreType.DMA
    half = jnp.bfloat16
    ways = 7 + 4 * (ys - 1)
    buffers = [
        pltpu.VMEM((slot_count, aux_here, size, size), half),
        pltpu.VMEM((slot_count, size, size), half),
        pltpu.VMEM((slot_count * shells, size), jnp.float32),
        pltpu.VMEM((atoms * per, size, occ), half),
        pltpu.SMEM((atoms * CAP,), jnp.int32),
        pltpu.SMEM((atoms * CAP,), jnp.int32),
        pltpu.VMEM((atoms * CAP, 8, 128), jnp.float32),
        pltpu.VMEM((planes * CAP, 8, 128), jnp.float32),
        pltpu.VMEM((chunks, planes, CAP, part, occ), half),
        pltpu.VMEM((chunks, planes, CAP, part, occ), half),
        pltpu.VMEM((chunks, planes, CAP, part, occ), half),
        pltpu.VMEM((planes, chunks, group, occ), half),
        pltpu.VMEM((planes, chunks, group, occ), half),
        pltpu.VMEM((planes + auxes - 1, chunks, group, occ), half),
        pltpu.VMEM((chunks, group, occ), half),
        pltpu.VMEM((2, auxes, chunks, group, occ), half),
        pltpu.VMEM((rows, auxes * aux_here * occ), half),
        pltpu.VMEM((auxes * kron_rows, auxes * kron_rows), half),
        pltpu.VMEM((split, group, rows), half),
        pltpu.VMEM((split, group, rows), half),
    ]
    semaphores = [
        dma((3,)),
        dma((atoms * 2,)),
        dma((3,)),
        dma((planes,)),
        dma((planes,)),
        dma((atoms,)),
        dma((2,)),
        dma((auxes,)),
        dma((auxes,)),
        dma((chunks,)),
        dma((chunks,)),
        dma((planes, chunks)),
        dma((planes, chunks)),
        dma((planes, chunks)),
        dma((planes, chunks)),
        dma((chunks,)),
        dma((planes, chunks)),
        dma((planes, chunks)),
        dma((planes, chunks)),
        dma((planes, chunks)),
        dma((auxes, chunks)),
        dma((ways, chunks)),
        dma((2, auxes, chunks)),
        dma((split,)),
        dma((split,)),
    ]
    return buffers, semaphores


VMEM_LIMIT = 60 * 1024 * 1024
STRIP = 16
SPLIT = 2


def fused_plan(planes, auxes, three_index, pair_mask, coefficients):
    slot_count, aux_here, size, _ = three_index.shape
    rows, occ = coefficients.shape
    per, shells = rows // size, pair_mask.shape[1]
    if planes != auxes or per % 2 or per > 8 or size % (32 * SPLIT) or shells % 8:
        return None
    buffers, semaphores = fused_scratch(
        planes, auxes, SPLIT, slot_count, aux_here, size, occ, per, shells, aux_here * STRIP
    )
    held = rows * 2 * rows * 4 + 2 * rows * occ * 2
    for ref in buffers:
        held += math.prod(ref.shape) * jnp.dtype(ref.dtype).itemsize
    if held > VMEM_LIMIT - 4 * 1024 * 1024:
        return None
    return buffers + semaphores


def fused_call(plan, planes, auxes, three_index, pair_mask, owners, subs, nus, live, coefficients, fit_rows):
    slot_count, aux_here, size, _ = three_index.shape
    rows, occ = coefficients.shape
    shells = pair_mask.shape[1]
    total_aux = fit_rows.shape[1]
    width = jnp.repeat(jnp.repeat(fit_rows, STRIP, 0), STRIP, 1)
    row = lax.broadcasted_iota(jnp.int32, width.shape, 0) % STRIP
    col = lax.broadcasted_iota(jnp.int32, width.shape, 1) % STRIP
    kron_rows = jnp.where(row == col, width, jnp.zeros_like(width))
    smem = pl.BlockSpec(memory_space=pltpu.SMEM)
    vmem = pl.BlockSpec(memory_space=pltpu.VMEM)
    return pl.pallas_call(
        functools.partial(fused_kernel, planes, auxes, SPLIT),
        out_shape=jax.ShapeDtypeStruct((rows, 2 * rows), jnp.float32),
        in_specs=[smem] * 4 + [pl.BlockSpec(memory_space=pl.ANY)] + [vmem] * 3,
        out_specs=vmem,
        scratch_shapes=plan,
        compiler_params=pltpu.CompilerParams(
            collective_id=2, has_side_effects=True, vmem_limit_bytes=VMEM_LIMIT
        ),
    )(
        owners, subs, nus, live, three_index, pair_mask.reshape(slot_count * shells, shells),
        coefficients.reshape(rows // size, size, occ), kron_rows,
    )


def per_device(
    three_index, pair_mask, pair_owner, pair_sub, pair_nu, live_count, coefficients, fit_matrix
):
    slot_count, aux_here, block_size, _ = three_index.shape
    rows_here, occupied = coefficients.shape
    atom_count = lax.axis_size("atom")
    aux_total = fit_matrix.shape[1]
    planes, auxes = atom_count // 2, lax.axis_size("aux")
    plan = fused_plan(planes, auxes, three_index, pair_mask, coefficients)
    if plan is not None:
        total = fused_call(
            plan, planes, auxes, three_index, pair_mask, pair_owner[:, 0], pair_sub, pair_nu,
            live_count, coefficients, fit_matrix,
        )
        return total * (aux_total * occupied) ** (-0.5)
    shell_size = block_size // pair_mask.shape[1]
    expanded = jnp.repeat(jnp.repeat(pair_mask, shell_size, 1), shell_size, 2).astype(jnp.bfloat16)
    owners = pair_owner[:, 0]
    ahead = jnp.arange(slot_count)[None, :] < jnp.arange(slot_count)[:, None]
    rank_within = jnp.sum(((owners[:, None] == owners[None, :]) & ahead).astype(jnp.int32), 1)
    placement = owners * CAP + rank_within
    routing = (jnp.arange(atom_count * CAP)[:, None] == placement[None, :]).astype(jnp.int32)
    slots = jnp.arange(slot_count, dtype=jnp.int32)

    def placed(values):
        return jnp.sum(routing * values[None, :], 1)

    live_codes = placed(jnp.where(slots < live_count[0], pair_sub + 1, 0))
    blocks = jnp.arange(rows_here // block_size)
    hits = (live_codes[:, None] == blocks[None, :] + 1).astype(jnp.float32)
    hits = hits.reshape(atom_count, CAP, blocks.shape[0], 1, 1)
    local_rows = route_call(
        placed(slots),
        placed(pair_nu),
        three_index,
        expanded,
        jnp.broadcast_to(hits, hits.shape[:3] + (8, 128)),
        coefficients,
    )
    total = exchange_call(local_rows, fit_matrix.astype(jnp.float32))
    return total * (aux_total * occupied) ** (-0.5)


def solution(mesh):
    in_specs = (
        P("atom", "aux", None, None),
        P("atom", None, None),
        P("atom", None),
        P("atom"),
        P("atom"),
        P("atom"),
        P("atom", None),
        P("aux", None),
    )
    out_specs = P("atom", "aux")
    return jax.shard_map(
        per_device, mesh=mesh, in_specs=in_specs, out_specs=out_specs, check_vma=False
    )
```

```python
import functools
import math

import jax
import jax.numpy as jnp
from jax import lax
from jax.experimental import pallas as pl
from jax.experimental.pallas import tpu as pltpu
from jax.sharding import PartitionSpec as P

CAP = 2
MESH = pl.DeviceIdType.MESH


def exchange_kernel(
    atoms, auxes, h_ref, fit_ref, out_ref,
    hall, hx, g, epart, cbuf, ybuf,
    local_sem, sx, sz0, sz, rh, sa, ra, sc, rc, sy, ry,
):
    planes, ys = atoms // 2, auxes // 2
    aux_here, rows, occ = h_ref.shape
    me = lax.axis_index("atom")
    ax = lax.axis_index("aux")
    hi, lo = me // 2, me % 2
    y, c = ax // 2, ax % 2
    partner = {"atom": hi * 2 + 1 - lo, "aux": ax}
    peer = {"atom": me, "aux": y * 2 + 1 - c}

    barrier = pltpu.get_barrier_semaphore()

    def greet(device):
        pl.semaphore_signal(barrier, inc=1, device_id=device, device_id_type=MESH)

    greet(partner)
    greet(peer)
    for d in range(1, ys):
        greet({"atom": me, "aux": ((y + d) % ys) * 2 + c})

    @pl.when(hi > 0)
    def _():
        greet({"atom": me - 2, "aux": ax})

    @pl.when(hi < planes - 1)
    def _():
        greet({"atom": me + 2, "aux": ax})

    before = jnp.minimum(hi, 1)
    behind = jnp.minimum(planes - 1 - hi, 1)
    pl.semaphore_wait(barrier, 1 + ys + before + behind)

    def remote(src, dst, send, recv, device):
        return pltpu.make_async_remote_copy(
            src_ref=src, dst_ref=dst, send_sem=send, recv_sem=recv,
            device_id=device, device_id_type=MESH,
        )

    def to_partner(k, atom, src):
        return remote(src, hall.at[atom], sx.at[k], rh.at[atom], partner)

    def along(atom, src, sem, step):
        return remote(src, hall.at[atom], sem, rh.at[atom], {"atom": me + 2 * step, "aux": ax})

    left_ok, right_ok = hi > 0, hi < planes - 1

    @pl.when(left_ok)
    def _():
        along(me, h_ref, sz0.at[0], -1).start()

    @pl.when(right_ok)
    def _():
        along(me, h_ref, sz0.at[1], 1).start()

    to_partner(0, me, h_ref).start()
    for d in range(1, ys):
        remote(h_ref, hx.at[ax], sa.at[d], ra.at[ax], {"atom": me, "aux": ((y + d) % ys) * 2 + c}).start()
    remote(h_ref, hx.at[ax], sa.at[0], ra.at[ax], peer).start()
    own = pltpu.make_async_copy(h_ref, hall.at[me], local_sem.at[0])
    own.start()
    own_aux = pltpu.make_async_copy(h_ref, hx.at[ax], local_sem.at[1])
    own_aux.start()

    def plane_of(k):
        half = (k + 1) // 2
        return hi + half * (1 - 2 * (k % 2))

    def valid(k):
        p = plane_of(k)
        return (p >= 0) & (p < planes) & (k < 2 * planes - 1)

    def forward_ok(k):
        target = hi - (1 - 2 * (k % 2))
        return valid(k) & (target >= 0) & (target < planes)

    def wait_block(atom):
        remote(h_ref, hall.at[atom], sx.at[0], rh.at[atom], partner).wait_recv()

    def relay(k):
        @pl.when(valid(k))
        def _():
            atom = plane_of(k) * 2 + lo
            wait_block(atom)

            @pl.when(forward_ok(k))
            def _():
                along(atom, hall.at[atom], sz.at[k], -(1 - 2 * (k % 2))).start()

            to_partner(k, atom, hall.at[atom]).start()

    relay(1)
    relay(2)

    for d in range(1, ys):
        src = ((y + d) % ys) * 2 + c
        remote(h_ref, hx.at[src], sa.at[0], ra.at[src], peer).wait_recv()
        remote(hx.at[src], hx.at[src], sa.at[ys - 1 + d], ra.at[src], peer).start()
    for d in range(ys):
        src = ((y + d) % ys) * 2 + 1 - c
        remote(h_ref, hx.at[src], sa.at[0], ra.at[src], peer).wait_recv()
    own_aux.wait()
    own.wait()

    piece = 32

    @pl.loop(0, rows // piece)
    def _(j):
        at = pl.ds(pl.multiple_of(j * piece, piece), piece)
        sums = [jnp.zeros((piece, occ), jnp.float32) for _ in range(aux_here)]
        for p in range(aux_here * auxes):
            block = hx[p // aux_here, p % aux_here, at, :].astype(jnp.float32)
            for q in range(aux_here):
                sums[q] = sums[q] + fit_ref[q, p] * block
        for q in range(aux_here):
            g[at, q * occ:(q + 1) * occ] = sums[q].astype(jnp.bfloat16)

    width = 256

    def product(k):
        p = plane_of(k)

        @pl.when(k > 0)
        def _():
            wait_block(p * 2 + 1 - lo)

        @pl.when(k == 0)
        def _():
            wait_block(hi * 2 + 1 - lo)

        for half in range(2):
            @pl.loop(0, rows // width)
            def _(j):
                at = pl.ds(pl.multiple_of(j * width, width), width)
                right = jnp.concatenate(
                    [hall[p * 2 + half, q, at, :] for q in range(aux_here)], axis=-1
                )
                part = lax.dot_general(
                    g[...], right, (((1,), (1,)), ((), ())), preferred_element_type=jnp.float32
                )
                col = pl.ds(pl.multiple_of(half * rows + j * width, width), width)
                epart[p, :, col] = part.astype(jnp.bfloat16)

        @pl.when(p % 2 != c)
        def _():
            remote(epart.at[p], cbuf.at[p // 2], sc.at[p // 2], rc.at[p // 2], peer).start()

    def join(k):
        p = plane_of(k)
        yt = p // 2

        @pl.when(p % 2 == c)
        def _():
            remote(epart.at[p], cbuf.at[yt], sc.at[yt], rc.at[yt], peer).wait_recv()

            @pl.when(yt != y)
            def _():
                @pl.loop(0, rows // 64)
                def _(j):
                    at = pl.ds(pl.multiple_of(j * 64, 64), 64)
                    total = epart[p, at, :].astype(jnp.float32) + cbuf[yt, at, :].astype(jnp.float32)
                    epart[p, at, :] = total.astype(jnp.bfloat16)

                remote(epart.at[p], ybuf.at[y], sy.at[yt], ry.at[y], {"atom": me, "aux": p}).start()

    @pl.loop(0, 2 * planes)
    def _(k):
        @pl.when(valid(k))
        def _():
            product(k)

        @pl.when(k > 0)
        def _():
            @pl.when(valid(k - 1))
            def _():
                join(k - 1)

        relay(k + 3)

    for d in range(1, ys):
        src = (y + d) % ys
        remote(epart.at[ax], ybuf.at[src], sy.at[src], ry.at[src], peer).wait_recv()

    @pl.loop(0, rows // 64)
    def _(j):
        at = pl.ds(pl.multiple_of(j * 64, 64), 64)
        total = epart[ax, at, :].astype(jnp.float32) + cbuf[y, at, :].astype(jnp.float32)
        for d in range(1, ys):
            total = total + ybuf[(y + d) % ys, at, :].astype(jnp.float32)
        out_ref[at, :] = total

    @pl.when(left_ok)
    def _():
        along(me, h_ref, sz0.at[0], -1).wait_send()

    @pl.when(right_ok)
    def _():
        along(me, h_ref, sz0.at[1], 1).wait_send()

    for k in range(2 * planes - 1):
        @pl.when(valid(k))
        def _():
            to_partner(k, me, h_ref).wait_send()

            if k > 0:
                @pl.when(forward_ok(k))
                def _():
                    along(me, h_ref, sz.at[k], -(1 - 2 * (k % 2))).wait_send()

    for d in range(2 * ys - 1):
        remote(h_ref, hx.at[ax], sa.at[d], ra.at[ax], peer).wait_send()
    for t in range(ys):
        remote(epart.at[ax], cbuf.at[t], sc.at[t], rc.at[t], peer).wait_send()
    for d in range(1, ys):
        remote(epart.at[ax], ybuf.at[y], sy.at[(y + d) % ys], ry.at[y], peer).wait_send()


def exchange_call(h, fit_rows):
    aux_here, rows, occ = h.shape
    atoms, auxes = lax.axis_size("atom"), lax.axis_size("aux")
    planes, ys = atoms // 2, auxes // 2
    columns = rows * atoms // auxes
    dma = pltpu.SemaphoreType.DMA
    return pl.pallas_call(
        functools.partial(exchange_kernel, atoms, auxes),
        out_shape=jax.ShapeDtypeStruct((rows, columns), jnp.float32),
        in_specs=[
            pl.BlockSpec(memory_space=pltpu.VMEM),
            pl.BlockSpec(memory_space=pltpu.SMEM),
        ],
        out_specs=pl.BlockSpec(memory_space=pltpu.VMEM),
        scratch_shapes=[
            pltpu.VMEM((atoms, aux_here, rows, occ), jnp.bfloat16),
            pltpu.VMEM((auxes, aux_here, rows, occ), jnp.bfloat16),
            pltpu.VMEM((rows, aux_here * occ), jnp.bfloat16),
            pltpu.VMEM((auxes, rows, columns), jnp.bfloat16),
            pltpu.VMEM((ys, rows, columns), jnp.bfloat16),
            pltpu.VMEM((ys, rows, columns), jnp.bfloat16),
            dma((2,)),
            dma((2 * planes - 1,)),
            dma((2,)),
            dma((2 * planes - 1,)),
            dma((atoms,)),
            dma((2 * ys - 1,)),
            dma((auxes,)),
            dma((ys,)),
            dma((ys,)),
            dma((ys,)),
            dma((ys,)),
        ],
        compiler_params=pltpu.CompilerParams(
            collective_id=0, has_side_effects=True, vmem_limit_bytes=60 * 1024 * 1024
        ),
    )(h, fit_rows)


def route_kernel(
    atoms, order_ref, nu_ref, three_ref, mask_ref, code_ref, own_ref, out_ref,
    orbitals, outgoing, arrived, codes, acc, summed, landed,
    local_sem, sx, sz0, sz, rh, sd, rd, sk, rk, cross_sem,
):
    planes, middle = atoms // 2, atoms // 2
    cap = code_ref.shape[1]
    per, size, occ = own_ref.shape
    aux_here = three_ref.shape[1]
    share = aux_here // 2
    me = lax.axis_index("atom")
    ax = lax.axis_index("aux")
    hi, lo = me // 2, me % 2
    side, pos = me // middle, me % middle

    def at_atom(atom):
        return {"atom": atom, "aux": ax}

    barrier = pltpu.get_barrier_semaphore()
    for d in range(1, atoms):
        pl.semaphore_signal(
            barrier, inc=1, device_id=at_atom((me + d) % atoms), device_id_type=MESH
        )
    pl.semaphore_wait(barrier, atoms - 1)

    def remote(src, dst, send, recv, device):
        return pltpu.make_async_remote_copy(
            src_ref=src, dst_ref=dst, send_sem=send, recv_sem=recv,
            device_id=device, device_id_type=MESH,
        )

    def spot(atom):
        return orbitals.at[pl.ds(atom * per, per)]

    def to_partner(k, atom, src):
        return remote(src, spot(atom), sx.at[k], rh.at[atom], at_atom(hi * 2 + 1 - lo))

    def along(atom, src, sem, step):
        return remote(src, spot(atom), sem, rh.at[atom], at_atom(me + 2 * step))

    left_ok, right_ok = hi > 0, hi < planes - 1

    @pl.when(left_ok)
    def _():
        along(me, own_ref, sz0.at[0], -1).start()

    @pl.when(right_ok)
    def _():
        along(me, own_ref, sz0.at[1], 1).start()

    to_partner(0, me, own_ref).start()
    own = pltpu.make_async_copy(own_ref, spot(me), local_sem.at[0])
    own.start()

    def plane_of(k):
        half = (k + 1) // 2
        return hi + half * (1 - 2 * (k % 2))

    def valid(k):
        p = plane_of(k)
        return (p >= 0) & (p < planes)

    def forward_ok(k):
        target = hi - (1 - 2 * (k % 2))
        return valid(k) & (target >= 0) & (target < planes)

    def wait_block(atom):
        remote(own_ref, spot(atom), sx.at[0], rh.at[atom], at_atom(hi * 2 + 1 - lo)).wait_recv()

    @pl.loop(1, 2 * planes - 1)
    def _(k):
        @pl.when(valid(k))
        def _():
            atom = plane_of(k) * 2 + lo
            wait_block(atom)

            @pl.when(forward_ok(k))
            def _():
                along(atom, spot(atom), sz.at[k], -(1 - 2 * (k % 2))).start()

            to_partner(k, atom, spot(atom)).start()

    @pl.loop(0, planes)
    def _(p):
        wait_block(p * 2 + 1 - lo)

    own.wait()

    def half_block(place, part):
        slot, nu = order_ref[place], nu_ref[place]
        right = orbitals[nu]
        left = three_ref[slot, part * share:(part + 1) * share] * mask_ref[slot][None, :, :]
        value = jnp.dot(
            left.reshape(share * size, size), right, preferred_element_type=jnp.float32
        )
        return value.reshape(share, size, occ).astype(jnp.bfloat16)

    def target_of(j):
        return (pos + j % (middle - 1) + 1) % middle

    def block(part, j, lane, device):
        return remote(
            outgoing.at[part, j], arrived.at[part, lane], sd.at[part, j], rd.at[part, lane], device
        )

    def start_sends(first, owner_side, part):
        @pl.loop(first, first + middle - 1)
        def _(j):
            q = target_of(j)
            owner = owner_side * middle + q
            lane = (first // (middle - 1)) * middle + pos

            @pl.loop(0, cap)
            def _(r):
                outgoing[part, j, r] = half_block(owner * cap + r, part)

            device = at_atom(side * middle + q)
            if part == 0:
                remote(code_ref.at[owner], codes.at[lane], sk.at[j], rk.at[lane], device).start()
            block(part, j, lane, device).start()

    def fill_own(lane, owner, sem):
        @pl.loop(0, cap)
        def _(r):
            for part in range(2):
                arrived[part, lane, r] = half_block(owner * cap + r, part)

        keep = pltpu.make_async_copy(code_ref.at[owner], codes.at[lane], sem)
        keep.start()
        keep.wait()

    start_sends(0, 1 - side, 0)
    start_sends(0, 1 - side, 1)
    fill_own(pos, (1 - side) * middle + pos, local_sem.at[1])
    start_sends(middle - 1, side, 0)
    start_sends(middle - 1, side, 1)
    fill_own(middle + pos, me, local_sem.at[2])

    def take(src, part):
        hits = [
            [codes[src, r, b] for r in range(cap)]
            for b in range(per)
        ]

        @pl.loop(0, share * (size // 64))
        def _(n):
            p, row = n // (size // 64), n % (size // 64)
            at = pl.ds(pl.multiple_of(row * 64, 64), 64)
            values = [
                arrived[part, src, r, p, at, :].astype(jnp.float32).reshape(8, 8, occ)
                for r in range(cap)
            ]
            for b in range(per):
                to = pl.ds(pl.multiple_of(b * size + row * 64, 64), 64)
                total = acc[part * share + p, to, :].reshape(8, 8, occ)
                for r in range(cap):
                    total = total + values[r] * hits[b][r][None]
                acc[part * share + p, to, :] = total.reshape(64, occ)

    def take_all(base, part):
        span = pl.ds(part * share, share)
        acc[span] = jnp.zeros((share,) + acc.shape[1:], jnp.float32)
        take(base + pos, part)

        @pl.loop(1, middle)
        def _(i):
            src = (pos + middle - i) % middle
            lane = base + src
            device = at_atom(side * middle + src)
            if part == 0:
                remote(code_ref.at[0], codes.at[lane], sk.at[0], rk.at[lane], device).wait_recv()
            block(part, 0, lane, device).wait_recv()
            take(lane, part)

    across = at_atom((1 - side) * middle + pos)
    crossings = []
    for part in range(2):
        take_all(0, part)
        span = pl.ds(part * share, share)
        summed[span] = acc[span].astype(jnp.bfloat16)
        cross = remote(
            summed.at[span], landed.at[span], cross_sem.at[part], cross_sem.at[2 + part], across
        )
        cross.start()
        crossings.append(cross)
    take_all(middle, 0)
    take_all(middle, 1)
    for part in range(2):
        crossings[part].wait_recv()
        span = pl.ds(part * share, share)
        out_ref[span] = (acc[span] + landed[span].astype(jnp.float32)).astype(jnp.bfloat16)
    for cross in crossings:
        cross.wait_send()

    @pl.when(left_ok)
    def _():
        along(me, own_ref, sz0.at[0], -1).wait_send()

    @pl.when(right_ok)
    def _():
        along(me, own_ref, sz0.at[1], 1).wait_send()

    to_partner(0, me, own_ref).wait_send()

    @pl.loop(1, 2 * planes - 1)
    def _(k):
        @pl.when(valid(k))
        def _():
            to_partner(k, me, own_ref).wait_send()

            @pl.when(forward_ok(k))
            def _():
                along(me, own_ref, sz.at[k], -(1 - 2 * (k % 2))).wait_send()

    @pl.loop(0, 2 * middle - 2)
    def _(j):
        device = at_atom(side * middle + target_of(j))
        block(0, j, 0, device).wait_send()
        block(1, j, 0, device).wait_send()
        remote(code_ref.at[0], codes.at[0], sk.at[j], rk.at[0], device).wait_send()


def route_call(order, nu, three_index, mask, codes, coefficients):
    aux_here, size = three_index.shape[1], three_index.shape[2]
    rows, occ = coefficients.shape
    per = rows // size
    atoms = lax.axis_size("atom")
    planes = atoms // 2
    dma = pltpu.SemaphoreType.DMA
    smem = pl.BlockSpec(memory_space=pltpu.SMEM)
    vmem = pl.BlockSpec(memory_space=pltpu.VMEM)
    return pl.pallas_call(
        functools.partial(route_kernel, atoms),
        out_shape=jax.ShapeDtypeStruct((aux_here, rows, occ), jnp.bfloat16),
        in_specs=[smem, smem, vmem, vmem, vmem, vmem],
        out_specs=vmem,
        scratch_shapes=[
            pltpu.VMEM((atoms * per, size, occ), jnp.bfloat16),
            pltpu.VMEM((2, atoms - 2, CAP, aux_here // 2, size, occ), jnp.bfloat16),
            pltpu.VMEM((2, atoms, CAP, aux_here // 2, size, occ), jnp.bfloat16),
            pltpu.VMEM((atoms, CAP, per, 8, 128), jnp.float32),
            pltpu.VMEM((aux_here, rows, occ), jnp.float32),
            pltpu.VMEM((aux_here, rows, occ), jnp.bfloat16),
            pltpu.VMEM((aux_here, rows, occ), jnp.bfloat16),
            dma((3,)),
            dma((2 * planes - 1,)),
            dma((2,)),
            dma((2 * planes - 1,)),
            dma((atoms,)),
            dma((2, atoms - 2)),
            dma((2, atoms)),
            dma((atoms - 2,)),
            dma((atoms,)),
            dma((4,)),
        ],
        compiler_params=pltpu.CompilerParams(
            collective_id=1, has_side_effects=True, vmem_limit_bytes=60 * 1024 * 1024
        ),
    )(order, nu, three_index, mask, codes, coefficients.reshape(per, size, occ))


def fused_kernel(
    planes, auxes, split,
    owner_ref, sub_ref, nu_ref, live_ref, three_hbm, mask_ref, coef_ref, fit_ref, out_ref,
    kron_ref, three, mexp, mrows, orb, order, nus, hits, hits_in, keep, xs, xr, up, dn, zb, own_rows, rows_all, fitted, kron, cs, cr,
    local_sem, orb_recv, orb_own, orb_line, orb_x, orb_core, code_sem, kron_send, kron_recv,
    x_send, x_recv, up_send, up_recv, dn_send, dn_recv,
    own_sem, line_up, line_dn, line_recv, b_send, b_recv, a_send, a_recv, c_send, c_recv,
):
    slot_count, aux_here, size, _ = three_hbm.shape
    per = coef_ref.shape[0]
    rows, occ = per * size, coef_ref.shape[2]
    atoms = planes * 2
    half = per // 2
    chunks, part = aux_here * split, size // split
    group = per * part
    shells = mask_ref.shape[1]
    shell = size // shells
    me = lax.axis_index("atom")
    ax = lax.axis_index("aux")
    z, x = me // 2, me % 2
    y, c = ax // 2, ax % 2
    ys = auxes // 2
    above, below = {"atom": me + 2, "aux": ax}, {"atom": me - 2, "aux": ax}
    partner = {"atom": z * 2 + 1 - x, "aux": ax}
    core = {"atom": me, "aux": y * 2 + 1 - c}
    has_up, has_dn = z < planes - 1, z > 0

    def at_aux(u):
        return {"atom": me, "aux": u}

    barrier = pltpu.get_barrier_semaphore()

    def greet(device):
        pl.semaphore_signal(barrier, inc=1, device_id=device, device_id_type=MESH)

    greet(partner)
    for d in range(1, auxes):
        greet(at_aux((ax + d) % auxes))

    @pl.when(has_up)
    def _():
        greet(above)

    @pl.when(has_dn)
    def _():
        greet(below)

    load_three = pltpu.make_async_copy(three_hbm, three, local_sem.at[0])
    load_three.start()
    load_orb = pltpu.make_async_copy(coef_ref, orb.at[pl.ds(me * per, per)], local_sem.at[2])
    load_orb.start()

    pl.semaphore_wait(
        barrier, auxes + jnp.minimum(z, 1) + jnp.minimum(planes - 1 - z, 1)
    )

    def remote(src, dst, send, recv, device):
        return pltpu.make_async_remote_copy(
            src_ref=src, dst_ref=dst, send_sem=send, recv_sem=recv,
            device_id=device, device_id_type=MESH,
        )

    def spot(atom, part):
        return orb.at[pl.ds(atom * per + part * half, half)]

    own_part = coef_ref.at[pl.ds(c * half, half)]

    def orb_copy(src, atom, part, send, device):
        return remote(src, spot(atom, part), send, orb_recv.at[atom * 2 + part], device)

    @pl.when(has_up)
    def _():
        orb_copy(own_part, me, c, orb_own.at[0], above).start()

    @pl.when(has_dn)
    def _():
        orb_copy(own_part, me, c, orb_own.at[1], below).start()

    orb_copy(own_part, me, c, orb_own.at[2], partner).start()

    def wait_orb(atom, part):
        orb_copy(own_part, atom, part, orb_own.at[0], partner).wait_recv()

    lane_row = lax.broadcasted_iota(jnp.int32, (8, 128), 0)
    live = live_ref[0]

    @pl.loop(0, atoms)
    def _(o):
        def scan(s, carry):
            count, slots, nu, codes = carry
            hit = owner_ref[s] == o
            code = jnp.where(s < live, sub_ref[s] + 1, 0)
            new = []
            for r in range(CAP):
                take = hit & (count == r)
                new.append((
                    jnp.where(take, s, slots[r]),
                    jnp.where(take, nu_ref[s], nu[r]),
                    jnp.where(take, code, codes[r]),
                ))
            count = count + jnp.where(hit, 1, 0)
            return count, tuple(v[0] for v in new), tuple(v[1] for v in new), tuple(v[2] for v in new)

        zero = jnp.int32(0)
        zeros = (zero,) * CAP
        _, slots, nu, codes = lax.fori_loop(0, slot_count, scan, (zero, zeros, zeros, zeros))
        for r in range(CAP):
            index = ((o % 2) * planes + o // 2) * CAP + r
            order[index] = slots[r]
            nus[index] = nu[r]
            hits[index] = jnp.where(lane_row == codes[r] - 1, 1.0, 0.0)

    code_count = planes * CAP
    send_codes = remote(
        hits.at[pl.ds((1 - x) * code_count, code_count)], hits_in, code_sem.at[0], code_sem.at[1], partner
    )
    send_codes.start()

    def iota(shape, dim):
        return lax.broadcasted_iota(jnp.int32, shape, dim)

    aux_total = auxes * aux_here
    strip = kron_ref.shape[0] // aux_here
    tall, wide = kron_ref.shape
    down = jnp.where(iota((tall, aux_here), 0) // strip == iota((tall, aux_here), 1), 1.0, 0.0)
    along = jnp.where(iota((aux_total, wide), 1) // strip == iota((aux_total, wide), 0), 1.0, 0.0)
    spread_rows = jnp.dot(down, fit_ref[...].astype(jnp.float32), preferred_element_type=jnp.float32)
    spread_all = jnp.dot(spread_rows, along, preferred_element_type=jnp.float32)
    same = iota((tall, wide), 0) % strip == iota((tall, wide), 1) % strip
    kron_ref[...] = jnp.where(same, spread_all, 0.0).astype(jnp.bfloat16)
    load_kron = pltpu.make_async_copy(
        kron_ref, kron.at[pl.ds(pl.multiple_of(ax * kron_ref.shape[0], kron_ref.shape[0]), kron_ref.shape[0])], local_sem.at[1]
    )
    load_kron.start()

    spread = jnp.where(
        lax.broadcasted_iota(jnp.int32, (shells, size), 1) // shell
        == lax.broadcasted_iota(jnp.int32, (shells, size), 0), 1.0, 0.0
    )
    for m in range(shells):
        mrows[m] = lax.dot_general(
            mask_ref[m].astype(jnp.float32), spread, (((0,), (0,)), ((), ())),
            preferred_element_type=jnp.float32,
        )

    @pl.loop(0, slot_count)
    def _(s):
        for m in range(shells):
            mexp[s, m * shell:(m + 1) * shell, :] = jnp.broadcast_to(
                mrows[m, pl.ds(s, 1), :], (shell, size)
            ).astype(jnp.bfloat16)

    def pass_orb(p, upward):
        atom = p * 2 + x
        wait_orb(atom, c)
        if upward:
            @pl.when(has_up)
            def _():
                orb_copy(spot(atom, c), atom, c, orb_line.at[p], above).start()
        else:
            @pl.when(has_dn)
            def _():
                orb_copy(spot(atom, c), atom, c, orb_line.at[p], below).start()
        orb_copy(spot(atom, c), atom, c, orb_x.at[p], partner).start()
        orb_copy(spot(atom, c), atom, c, orb_core.at[atom], core).start()

    def hand_orb(p):
        atom = p * 2 + 1 - x
        wait_orb(atom, c)
        orb_copy(spot(atom, c), atom, c, orb_core.at[atom], core).start()

    @pl.loop(1, planes)
    def _(d):
        @pl.when(z - d >= 0)
        def _():
            pass_orb(z - d, True)

        @pl.when(z + d < planes)
        def _():
            pass_orb(z + d, False)

    hand_orb(z)

    @pl.loop(1, planes)
    def _(d):
        @pl.when(z - d >= 0)
        def _():
            hand_orb(z - d)

        @pl.when(z + d < planes)
        def _():
            hand_orb(z + d)

    load_kron.wait()
    load_orb.wait()

    def kron_part(u):
        return kron.at[pl.ds(pl.multiple_of(u * kron_ref.shape[0], kron_ref.shape[0]), kron_ref.shape[0])]

    for d in range(1, auxes):
        remote(kron_ref, kron_part(ax), kron_send.at[d], kron_recv.at[ax], at_aux((ax + d) % auxes)).start()

    @pl.loop(0, planes)
    def _(p):
        wait_orb(p * 2 + 1 - x, 1 - c)

        @pl.when(p != z)
        def _():
            wait_orb(p * 2 + x, 1 - c)

    load_three.wait()
    send_codes.wait_recv()

    def half_block(index, k):
        slot, nu = order[index], nus[index]
        at = pl.ds(pl.multiple_of((k % split) * part, part), part)
        left = three[slot, k // split, at, :] * mexp[slot, at, :]
        return jnp.dot(left, orb[nu], preferred_element_type=jnp.float32).astype(jnp.bfloat16)

    def x_copy(k):
        return remote(xs.at[k], xr.at[k], x_send.at[k], x_recv.at[k], partner)

    def add_dense(p, k, extras, target):
        own_hits = [
            [jnp.broadcast_to(hits[(x * planes + p) * CAP + r, b:b + 1, :], (8, 128))[None] for r in range(CAP)]
            for b in range(per)
        ]
        in_hits = [
            [jnp.broadcast_to(hits_in[p * CAP + r, b:b + 1, :], (8, 128))[None] for r in range(CAP)]
            for b in range(per)
        ]
        shape = (part // 8, 8, occ)
        own = [keep[k, p, r].astype(jnp.float32).reshape(shape) for r in range(CAP)]
        other = [xr[k, p, r].astype(jnp.float32).reshape(shape) for r in range(CAP)]
        for b in range(per):
            to = slice(b * part, (b + 1) * part)
            total = own[0] * own_hits[b][0] + other[0] * in_hits[b][0]
            for r in range(1, CAP):
                total = total + own[r] * own_hits[b][r] + other[r] * in_hits[b][r]
            for extra in extras:
                total = total + extra[p, k, to, :].astype(jnp.float32).reshape(shape)
            value = total.reshape(part, occ).astype(jnp.bfloat16)
            if target is own_rows:
                target[k, to, :] = value
            else:
                target[p, k, to, :] = value

    def up_copy(p, k):
        ref = up.at[p, k]
        return remote(ref, ref, up_send.at[p, k], up_recv.at[p, k], above)

    def dn_copy(p, k):
        ref = dn.at[p, k]
        return remote(ref, ref, dn_send.at[p, k], dn_recv.at[p, k], below)

    def lane_of(p):
        return (p + 2 * planes - ax - 1) % planes

    def b_lane(sender, target):
        return planes - 1 + (sender + auxes - target) % auxes

    def line_copy(src, p, k, send, device):
        return remote(src, zb.at[lane_of(p), k], send, line_recv.at[p, k], device)

    def b_copy(src, p, k):
        return remote(src, zb.at[b_lane(ax, p), k], b_send.at[p, k], b_recv.at[ax, k], at_aux(p))

    def a_piece(column, u, k):
        return rows_all.at[column, u, k]

    def a_copy(column, u, k, which, device):
        ref = a_piece(column, u, k)
        return remote(ref, ref, a_send.at[which, k], a_recv.at[column, u, k], device)

    def own_a_copy(k, which, device):
        return remote(
            own_rows.at[k], a_piece(x, ax, k), a_send.at[which, k], a_recv.at[x, ax, k], device
        )

    def own_copy(k):
        return pltpu.make_async_copy(own_rows.at[k], a_piece(x, ax, k), own_sem.at[k])

    def y_devices():
        return [((y + d) % ys) * 2 + c for d in range(1, ys)]

    def inside(k):
        return (k >= 0) & (k < chunks)

    def reduce_rows(t, zz):
        if zz < planes - 1:
            ku = t - 1 - zz

            @pl.when(inside(ku))
            def _():
                for p in range(planes - 1, zz, -1):
                    if zz > 0:
                        up_copy(p, ku).wait_recv()
                    add_dense(p, ku, [up] if zz > 0 else [], up)
                    up_copy(p, ku).start()

        if zz > 0:
            kd = t - planes + zz

            @pl.when(inside(kd))
            def _():
                for p in range(zz):
                    if zz < planes - 1:
                        dn_copy(p, kd).wait_recv()
                    add_dense(p, kd, [dn] if zz < planes - 1 else [], dn)
                    dn_copy(p, kd).start()

        kh = t - 1 - max(zz, planes - 1 - zz)

        @pl.when(inside(kh))
        def _():
            extras = []
            if zz > 0:
                up_copy(zz, kh).wait_recv()
                extras.append(up)
            if zz < planes - 1:
                dn_copy(zz, kh).wait_recv()
                extras.append(dn)
            add_dense(zz, kh, extras, own_rows)
            mine = own_rows.at[kh]
            own_copy(kh).start()
            if zz < planes - 1:
                line_copy(mine, zz, kh, line_up.at[zz, kh], above).start()
            if zz > 0:
                line_copy(mine, zz, kh, line_dn.at[zz, kh], below).start()
            own_a_copy(kh, 0, partner).start()
            for n, u in enumerate(y_devices()):
                own_a_copy(kh, 7 + 2 * n, at_aux(u)).start()
            own_a_copy(kh, 1, core).start()

    def pass_line(t, zz, p):
        kz = t - 1 - max(p, planes - 1 - p) - abs(zz - p)

        @pl.when(inside(kz))
        def _():
            piece = zb.at[lane_of(p), kz]
            line_copy(piece, p, kz, line_up.at[p, kz], above).wait_recv()
            if p < zz < planes - 1:
                line_copy(piece, p, kz, line_up.at[p, kz], above).start()
            if p > zz > 0:
                line_copy(piece, p, kz, line_dn.at[p, kz], below).start()

            @pl.when(p != ax)
            def _():
                b_copy(piece, p, kz).start()

    def pass_rows(t, zz):
        ka = t - 2 - max(zz, planes - 1 - zz)

        @pl.when(inside(ka))
        def _():
            a_copy(1 - x, ax, ka, 0, partner).wait_recv()
            for n, u in enumerate(y_devices()):
                a_copy(1 - x, ax, ka, 8 + 2 * n, at_aux(u)).start()
            a_copy(1 - x, ax, ka, 2, core).start()
            for n, u in enumerate(y_devices()):
                a_copy(x, u, ka, 0, partner).wait_recv()
                a_copy(x, u, ka, 7 + 2 * (ys - 1) + 2 * n, core).start()

        kb = t - 3 - max(zz, planes - 1 - zz)

        @pl.when(inside(kb))
        def _():
            for n, u in enumerate(y_devices()):
                a_copy(1 - x, u, kb, 0, partner).wait_recv()
                a_copy(1 - x, u, kb, 8 + 2 * (ys - 1) + 2 * n, core).start()

        for d in range(1, planes):
            for p in (zz - d, zz + d):
                if 0 <= p < planes:
                    pass_line(t, zz, p)

    @pl.loop(0, chunks + 2 * planes - 1)
    def _(t):
        @pl.when(t < chunks)
        def _():
            @pl.loop(0, planes)
            def _(p):
                for r in range(CAP):
                    xs[t, p, r] = half_block(((1 - x) * planes + p) * CAP + r, t)

            x_copy(t).start()

            @pl.loop(0, planes)
            def _(p):
                for r in range(CAP):
                    keep[t, p, r] = half_block((x * planes + p) * CAP + r, t)

        @pl.when((t >= 1) & (t <= chunks))
        def _():
            x_copy(t - 1).wait_recv()

        for zz in range(planes):
            @pl.when(z == zz)
            def _():
                reduce_rows(t, zz)
                pass_rows(t, zz)

    for d in range(1, auxes):
        remote(kron_ref, kron_part((ax + d) % auxes), kron_send.at[d], kron_recv.at[(ax + d) % auxes], core).wait_recv()

    @pl.loop(0, chunks)
    def _(k):
        own_copy(k).wait()
        for d in range(ys):
            u = ((y + d) % ys) * 2 + 1 - c
            for column in range(2):
                a_copy(column, u, k, 0, partner).wait_recv()

        @pl.when(z != ax)
        def _():
            for d in range(1, auxes):
                u = (ax + d) % auxes
                remote(
                    zb.at[b_lane(u, ax), k], zb.at[b_lane(u, ax), k],
                    b_send.at[0, k], b_recv.at[u, k], core,
                ).wait_recv()

    total_aux = auxes * aux_here
    pairs = [(u, p) for u in range(auxes) for p in range(aux_here)]

    def mix(load):
        for h in range(split):
            @pl.loop(0, group // (2 * strip))
            def _(j):
                right = jnp.concatenate([
                    jnp.concatenate([
                        load(u, p * split + h, pl.ds(pl.multiple_of((2 * j + e) * strip, strip), strip))
                        for u, p in pairs
                    ], axis=0)
                    for e in range(2)
                ], axis=-1)
                value = jnp.dot(kron[...], right, preferred_element_type=jnp.float32).astype(jnp.bfloat16)
                for e in range(2):
                    place = (2 * j + e) * strip
                    to = (place // part) * size + h * part + place % part
                    to = pl.ds(pl.multiple_of(to, strip), strip)
                    for q in range(total_aux):
                        fitted[to, q * occ:(q + 1) * occ] = value[
                            q * strip:(q + 1) * strip, e * occ:(e + 1) * occ
                        ]

    @pl.when(z == ax)
    def _():
        mix(lambda u, k, at: rows_all[x, u, k, at, :])

    @pl.when(z != ax)
    def _():
        mix(lambda u, k, at: zb[b_lane(u, ax), k, at, :])

    def product(column, h):
        left = jnp.concatenate([rows_all[column, u, p * split + h] for u, p in pairs], axis=-1)
        return lax.dot_general(
            left, fitted[...], (((1,), (1,)), ((), ())), preferred_element_type=jnp.float32
        )

    def c_copy(h):
        return remote(cs.at[h], cr.at[h], c_send.at[h], c_recv.at[h], partner)

    def place_rows(h, column, value):
        for b in range(per):
            to = pl.ds(pl.multiple_of(b * size + h * part, part), part)
            out_ref[to, pl.ds(pl.multiple_of(column * rows, rows), rows)] = value[b * part:(b + 1) * part, :]

    @pl.loop(0, split)
    def _(h):
        cs[h] = product(1 - x, h).astype(jnp.bfloat16)
        c_copy(h).start()

    @pl.loop(0, split)
    def _(h):
        place_rows(h, x, product(x, h))

    @pl.loop(0, split)
    def _(h):
        c_copy(h).wait_recv()
        place_rows(h, 1 - x, cr[h].astype(jnp.float32))

    @pl.when(has_up)
    def _():
        orb_copy(own_part, me, c, orb_own.at[0], above).wait_send()

    @pl.when(has_dn)
    def _():
        orb_copy(own_part, me, c, orb_own.at[1], below).wait_send()

    orb_copy(own_part, me, c, orb_own.at[2], partner).wait_send()
    send_codes.wait_send()

    @pl.loop(0, planes)
    def _(p):
        @pl.when(p != z)
        def _():
            @pl.when(((p < z) & has_up) | ((p > z) & has_dn))
            def _():
                orb_copy(own_part, me, c, orb_line.at[p], partner).wait_send()

            orb_copy(own_part, me, c, orb_x.at[p], partner).wait_send()
            orb_copy(own_part, me, c, orb_core.at[p * 2 + x], partner).wait_send()

        orb_copy(own_part, me, c, orb_core.at[p * 2 + 1 - x], partner).wait_send()

    for d in range(1, auxes):
        remote(kron_ref, kron_part(ax), kron_send.at[d], kron_recv.at[ax], core).wait_send()

    @pl.loop(0, chunks)
    def _(k):
        x_copy(k).wait_send()
        for which in range(7 + 4 * (ys - 1)):
            if which < 3 or which >= 7:
                a_copy(x, ax, k, which, partner).wait_send()

        @pl.loop(0, planes)
        def _(p):
            @pl.when(p > z)
            def _():
                up_copy(p, k).wait_send()

            @pl.when(p < z)
            def _():
                dn_copy(p, k).wait_send()

            @pl.when((p <= z) & has_up)
            def _():
                line_copy(a_piece(x, ax, k), z, k, line_up.at[p, k], partner).wait_send()

            @pl.when((p >= z) & has_dn)
            def _():
                line_copy(a_piece(x, ax, k), z, k, line_dn.at[p, k], partner).wait_send()

            @pl.when((p != z) & (p != ax))
            def _():
                b_copy(a_piece(x, ax, k), p, k).wait_send()

    @pl.loop(0, split)
    def _(h):
        c_copy(h).wait_send()


def fused_scratch(planes, auxes, split, slot_count, aux_here, size, occ, per, shells, kron_rows):
    atoms, rows, chunks, ys = planes * 2, per * size, aux_here * split, auxes // 2
    part, group = size // split, rows // split
    dma = pltpu.SemaphoreType.DMA
    half = jnp.bfloat16
    ways = 7 + 4 * (ys - 1)
    buffers = [
        pltpu.VMEM((kron_rows, auxes * kron_rows), half),
        pltpu.VMEM((slot_count, aux_here, size, size), half),
        pltpu.VMEM((slot_count, size, size), half),
        pltpu.VMEM((shells, slot_count, size), jnp.float32),
        pltpu.VMEM((atoms * per, size, occ), half),
        pltpu.SMEM((atoms * CAP,), jnp.int32),
        pltpu.SMEM((atoms * CAP,), jnp.int32),
        pltpu.VMEM((atoms * CAP, 8, 128), jnp.float32),
        pltpu.VMEM((planes * CAP, 8, 128), jnp.float32),
        pltpu.VMEM((chunks, planes, CAP, part, occ), half),
        pltpu.VMEM((chunks, planes, CAP, part, occ), half),
        pltpu.VMEM((chunks, planes, CAP, part, occ), half),
        pltpu.VMEM((planes, chunks, group, occ), half),
        pltpu.VMEM((planes, chunks, group, occ), half),
        pltpu.VMEM((planes + auxes - 1, chunks, group, occ), half),
        pltpu.VMEM((chunks, group, occ), half),
        pltpu.VMEM((2, auxes, chunks, group, occ), half),
        pltpu.VMEM((rows, auxes * aux_here * occ), half),
        pltpu.VMEM((auxes * kron_rows, auxes * kron_rows), half),
        pltpu.VMEM((split, group, rows), half),
        pltpu.VMEM((split, group, rows), half),
    ]
    semaphores = [
        dma((3,)),
        dma((atoms * 2,)),
        dma((3,)),
        dma((planes,)),
        dma((planes,)),
        dma((atoms,)),
        dma((2,)),
        dma((auxes,)),
        dma((auxes,)),
        dma((chunks,)),
        dma((chunks,)),
        dma((planes, chunks)),
        dma((planes, chunks)),
        dma((planes, chunks)),
        dma((planes, chunks)),
        dma((chunks,)),
        dma((planes, chunks)),
        dma((planes, chunks)),
        dma((planes, chunks)),
        dma((planes, chunks)),
        dma((auxes, chunks)),
        dma((ways, chunks)),
        dma((2, auxes, chunks)),
        dma((split,)),
        dma((split,)),
    ]
    return buffers, semaphores


VMEM_LIMIT = 60 * 1024 * 1024
STRIP = 16
SPLIT = 2


def fused_plan(planes, auxes, three_index, pair_mask, coefficients):
    slot_count, aux_here, size, _ = three_index.shape
    rows, occ = coefficients.shape
    per, shells = rows // size, pair_mask.shape[1]
    if planes != auxes or per % 2 or per > 8 or size % (32 * SPLIT) or shells % 8:
        return None
    buffers, semaphores = fused_scratch(
        planes, auxes, SPLIT, slot_count, aux_here, size, occ, per, shells, aux_here * STRIP
    )
    held = rows * 2 * rows * 4 + 2 * rows * occ * 2
    for ref in buffers:
        held += math.prod(ref.shape) * jnp.dtype(ref.dtype).itemsize
    if held > VMEM_LIMIT - 4 * 1024 * 1024:
        return None
    return buffers + semaphores


def fused_call(plan, planes, auxes, three_index, pair_mask, owners, subs, nus, live, coefficients, fit_rows):
    slot_count, aux_here, size, _ = three_index.shape
    rows, occ = coefficients.shape
    shells = pair_mask.shape[1]
    smem = pl.BlockSpec(memory_space=pltpu.SMEM)
    vmem = pl.BlockSpec(memory_space=pltpu.VMEM)
    return pl.pallas_call(
        functools.partial(fused_kernel, planes, auxes, SPLIT),
        out_shape=jax.ShapeDtypeStruct((rows, 2 * rows), jnp.float32),
        in_specs=[smem] * 4 + [pl.BlockSpec(memory_space=pl.ANY)] + [vmem] * 3,
        out_specs=vmem,
        scratch_shapes=plan,
        compiler_params=pltpu.CompilerParams(
            collective_id=2, has_side_effects=True, vmem_limit_bytes=VMEM_LIMIT
        ),
    )(
        owners, subs, nus, live, three_index, pair_mask.transpose(1, 2, 0),
        coefficients.reshape(rows // size, size, occ), fit_rows,
    )


def per_device(
    three_index, pair_mask, pair_owner, pair_sub, pair_nu, live_count, coefficients, fit_matrix
):
    slot_count, aux_here, block_size, _ = three_index.shape
    rows_here, occupied = coefficients.shape
    atom_count = lax.axis_size("atom")
    aux_total = fit_matrix.shape[1]
    planes, auxes = atom_count // 2, lax.axis_size("aux")
    plan = fused_plan(planes, auxes, three_index, pair_mask, coefficients)
    if plan is not None:
        total = fused_call(
            plan, planes, auxes, three_index, pair_mask, pair_owner[:, 0], pair_sub, pair_nu,
            live_count, coefficients, fit_matrix,
        )
        return total * (aux_total * occupied) ** (-0.5)
    shell_size = block_size // pair_mask.shape[1]
    expanded = jnp.repeat(jnp.repeat(pair_mask, shell_size, 1), shell_size, 2).astype(jnp.bfloat16)
    owners = pair_owner[:, 0]
    ahead = jnp.arange(slot_count)[None, :] < jnp.arange(slot_count)[:, None]
    rank_within = jnp.sum(((owners[:, None] == owners[None, :]) & ahead).astype(jnp.int32), 1)
    placement = owners * CAP + rank_within
    routing = (jnp.arange(atom_count * CAP)[:, None] == placement[None, :]).astype(jnp.int32)
    slots = jnp.arange(slot_count, dtype=jnp.int32)

    def placed(values):
        return jnp.sum(routing * values[None, :], 1)

    live_codes = placed(jnp.where(slots < live_count[0], pair_sub + 1, 0))
    blocks = jnp.arange(rows_here // block_size)
    hits = (live_codes[:, None] == blocks[None, :] + 1).astype(jnp.float32)
    hits = hits.reshape(atom_count, CAP, blocks.shape[0], 1, 1)
    local_rows = route_call(
        placed(slots),
        placed(pair_nu),
        three_index,
        expanded,
        jnp.broadcast_to(hits, hits.shape[:3] + (8, 128)),
        coefficients,
    )
    total = exchange_call(local_rows, fit_matrix.astype(jnp.float32))
    return total * (aux_total * occupied) ** (-0.5)


def solution(mesh):
    in_specs = (
        P("atom", "aux", None, None),
        P("atom", None, None),
        P("atom", None),
        P("atom"),
        P("atom"),
        P("atom"),
        P("atom", None),
        P("aux", None),
    )
    out_specs = P("atom", "aux")
    return jax.shard_map(
        per_device, mesh=mesh, in_specs=in_specs, out_specs=out_specs, check_vma=False
    )
```

```python
import functools
import math

import jax
import jax.numpy as jnp
from jax import lax
from jax.experimental import pallas as pl
from jax.experimental.pallas import tpu as pltpu
from jax.sharding import PartitionSpec as P

CAP = 2
MESH = pl.DeviceIdType.MESH


def exchange_kernel(
    atoms, auxes, h_ref, fit_ref, out_ref,
    hall, hx, g, epart, cbuf, ybuf,
    local_sem, sx, sz0, sz, rh, sa, ra, sc, rc, sy, ry,
):
    planes, ys = atoms // 2, auxes // 2
    aux_here, rows, occ = h_ref.shape
    me = lax.axis_index("atom")
    ax = lax.axis_index("aux")
    hi, lo = me // 2, me % 2
    y, c = ax // 2, ax % 2
    partner = {"atom": hi * 2 + 1 - lo, "aux": ax}
    peer = {"atom": me, "aux": y * 2 + 1 - c}

    barrier = pltpu.get_barrier_semaphore()

    def greet(device):
        pl.semaphore_signal(barrier, inc=1, device_id=device, device_id_type=MESH)

    greet(partner)
    greet(peer)
    for d in range(1, ys):
        greet({"atom": me, "aux": ((y + d) % ys) * 2 + c})

    @pl.when(hi > 0)
    def _():
        greet({"atom": me - 2, "aux": ax})

    @pl.when(hi < planes - 1)
    def _():
        greet({"atom": me + 2, "aux": ax})

    before = jnp.minimum(hi, 1)
    behind = jnp.minimum(planes - 1 - hi, 1)
    pl.semaphore_wait(barrier, 1 + ys + before + behind)

    def remote(src, dst, send, recv, device):
        return pltpu.make_async_remote_copy(
            src_ref=src, dst_ref=dst, send_sem=send, recv_sem=recv,
            device_id=device, device_id_type=MESH,
        )

    def to_partner(k, atom, src):
        return remote(src, hall.at[atom], sx.at[k], rh.at[atom], partner)

    def along(atom, src, sem, step):
        return remote(src, hall.at[atom], sem, rh.at[atom], {"atom": me + 2 * step, "aux": ax})

    left_ok, right_ok = hi > 0, hi < planes - 1

    @pl.when(left_ok)
    def _():
        along(me, h_ref, sz0.at[0], -1).start()

    @pl.when(right_ok)
    def _():
        along(me, h_ref, sz0.at[1], 1).start()

    to_partner(0, me, h_ref).start()
    for d in range(1, ys):
        remote(h_ref, hx.at[ax], sa.at[d], ra.at[ax], {"atom": me, "aux": ((y + d) % ys) * 2 + c}).start()
    remote(h_ref, hx.at[ax], sa.at[0], ra.at[ax], peer).start()
    own = pltpu.make_async_copy(h_ref, hall.at[me], local_sem.at[0])
    own.start()
    own_aux = pltpu.make_async_copy(h_ref, hx.at[ax], local_sem.at[1])
    own_aux.start()

    def plane_of(k):
        half = (k + 1) // 2
        return hi + half * (1 - 2 * (k % 2))

    def valid(k):
        p = plane_of(k)
        return (p >= 0) & (p < planes) & (k < 2 * planes - 1)

    def forward_ok(k):
        target = hi - (1 - 2 * (k % 2))
        return valid(k) & (target >= 0) & (target < planes)

    def wait_block(atom):
        remote(h_ref, hall.at[atom], sx.at[0], rh.at[atom], partner).wait_recv()

    def relay(k):
        @pl.when(valid(k))
        def _():
            atom = plane_of(k) * 2 + lo
            wait_block(atom)

            @pl.when(forward_ok(k))
            def _():
                along(atom, hall.at[atom], sz.at[k], -(1 - 2 * (k % 2))).start()

            to_partner(k, atom, hall.at[atom]).start()

    relay(1)
    relay(2)

    for d in range(1, ys):
        src = ((y + d) % ys) * 2 + c
        remote(h_ref, hx.at[src], sa.at[0], ra.at[src], peer).wait_recv()
        remote(hx.at[src], hx.at[src], sa.at[ys - 1 + d], ra.at[src], peer).start()
    for d in range(ys):
        src = ((y + d) % ys) * 2 + 1 - c
        remote(h_ref, hx.at[src], sa.at[0], ra.at[src], peer).wait_recv()
    own_aux.wait()
    own.wait()

    piece = 32

    @pl.loop(0, rows // piece)
    def _(j):
        at = pl.ds(pl.multiple_of(j * piece, piece), piece)
        sums = [jnp.zeros((piece, occ), jnp.float32) for _ in range(aux_here)]
        for p in range(aux_here * auxes):
            block = hx[p // aux_here, p % aux_here, at, :].astype(jnp.float32)
            for q in range(aux_here):
                sums[q] = sums[q] + fit_ref[q, p] * block
        for q in range(aux_here):
            g[at, q * occ:(q + 1) * occ] = sums[q].astype(jnp.bfloat16)

    width = 256

    def product(k):
        p = plane_of(k)

        @pl.when(k > 0)
        def _():
            wait_block(p * 2 + 1 - lo)

        @pl.when(k == 0)
        def _():
            wait_block(hi * 2 + 1 - lo)

        for half in range(2):
            @pl.loop(0, rows // width)
            def _(j):
                at = pl.ds(pl.multiple_of(j * width, width), width)
                right = jnp.concatenate(
                    [hall[p * 2 + half, q, at, :] for q in range(aux_here)], axis=-1
                )
                part = lax.dot_general(
                    g[...], right, (((1,), (1,)), ((), ())), preferred_element_type=jnp.float32
                )
                col = pl.ds(pl.multiple_of(half * rows + j * width, width), width)
                epart[p, :, col] = part.astype(jnp.bfloat16)

        @pl.when(p % 2 != c)
        def _():
            remote(epart.at[p], cbuf.at[p // 2], sc.at[p // 2], rc.at[p // 2], peer).start()

    def join(k):
        p = plane_of(k)
        yt = p // 2

        @pl.when(p % 2 == c)
        def _():
            remote(epart.at[p], cbuf.at[yt], sc.at[yt], rc.at[yt], peer).wait_recv()

            @pl.when(yt != y)
            def _():
                @pl.loop(0, rows // 64)
                def _(j):
                    at = pl.ds(pl.multiple_of(j * 64, 64), 64)
                    total = epart[p, at, :].astype(jnp.float32) + cbuf[yt, at, :].astype(jnp.float32)
                    epart[p, at, :] = total.astype(jnp.bfloat16)

                remote(epart.at[p], ybuf.at[y], sy.at[yt], ry.at[y], {"atom": me, "aux": p}).start()

    @pl.loop(0, 2 * planes)
    def _(k):
        @pl.when(valid(k))
        def _():
            product(k)

        @pl.when(k > 0)
        def _():
            @pl.when(valid(k - 1))
            def _():
                join(k - 1)

        relay(k + 3)

    for d in range(1, ys):
        src = (y + d) % ys
        remote(epart.at[ax], ybuf.at[src], sy.at[src], ry.at[src], peer).wait_recv()

    @pl.loop(0, rows // 64)
    def _(j):
        at = pl.ds(pl.multiple_of(j * 64, 64), 64)
        total = epart[ax, at, :].astype(jnp.float32) + cbuf[y, at, :].astype(jnp.float32)
        for d in range(1, ys):
            total = total + ybuf[(y + d) % ys, at, :].astype(jnp.float32)
        out_ref[at, :] = total

    @pl.when(left_ok)
    def _():
        along(me, h_ref, sz0.at[0], -1).wait_send()

    @pl.when(right_ok)
    def _():
        along(me, h_ref, sz0.at[1], 1).wait_send()

    for k in range(2 * planes - 1):
        @pl.when(valid(k))
        def _():
            to_partner(k, me, h_ref).wait_send()

            if k > 0:
                @pl.when(forward_ok(k))
                def _():
                    along(me, h_ref, sz.at[k], -(1 - 2 * (k % 2))).wait_send()

    for d in range(2 * ys - 1):
        remote(h_ref, hx.at[ax], sa.at[d], ra.at[ax], peer).wait_send()
    for t in range(ys):
        remote(epart.at[ax], cbuf.at[t], sc.at[t], rc.at[t], peer).wait_send()
    for d in range(1, ys):
        remote(epart.at[ax], ybuf.at[y], sy.at[(y + d) % ys], ry.at[y], peer).wait_send()


def exchange_call(h, fit_rows):
    aux_here, rows, occ = h.shape
    atoms, auxes = lax.axis_size("atom"), lax.axis_size("aux")
    planes, ys = atoms // 2, auxes // 2
    columns = rows * atoms // auxes
    dma = pltpu.SemaphoreType.DMA
    return pl.pallas_call(
        functools.partial(exchange_kernel, atoms, auxes),
        out_shape=jax.ShapeDtypeStruct((rows, columns), jnp.float32),
        in_specs=[
            pl.BlockSpec(memory_space=pltpu.VMEM),
            pl.BlockSpec(memory_space=pltpu.SMEM),
        ],
        out_specs=pl.BlockSpec(memory_space=pltpu.VMEM),
        scratch_shapes=[
            pltpu.VMEM((atoms, aux_here, rows, occ), jnp.bfloat16),
            pltpu.VMEM((auxes, aux_here, rows, occ), jnp.bfloat16),
            pltpu.VMEM((rows, aux_here * occ), jnp.bfloat16),
            pltpu.VMEM((auxes, rows, columns), jnp.bfloat16),
            pltpu.VMEM((ys, rows, columns), jnp.bfloat16),
            pltpu.VMEM((ys, rows, columns), jnp.bfloat16),
            dma((2,)),
            dma((2 * planes - 1,)),
            dma((2,)),
            dma((2 * planes - 1,)),
            dma((atoms,)),
            dma((2 * ys - 1,)),
            dma((auxes,)),
            dma((ys,)),
            dma((ys,)),
            dma((ys,)),
            dma((ys,)),
        ],
        compiler_params=pltpu.CompilerParams(
            collective_id=0, has_side_effects=True, vmem_limit_bytes=60 * 1024 * 1024
        ),
    )(h, fit_rows)


def route_kernel(
    atoms, order_ref, nu_ref, three_ref, mask_ref, code_ref, own_ref, out_ref,
    orbitals, outgoing, arrived, codes, acc, summed, landed,
    local_sem, sx, sz0, sz, rh, sd, rd, sk, rk, cross_sem,
):
    planes, middle = atoms // 2, atoms // 2
    cap = code_ref.shape[1]
    per, size, occ = own_ref.shape
    aux_here = three_ref.shape[1]
    share = aux_here // 2
    me = lax.axis_index("atom")
    ax = lax.axis_index("aux")
    hi, lo = me // 2, me % 2
    side, pos = me // middle, me % middle

    def at_atom(atom):
        return {"atom": atom, "aux": ax}

    barrier = pltpu.get_barrier_semaphore()
    for d in range(1, atoms):
        pl.semaphore_signal(
            barrier, inc=1, device_id=at_atom((me + d) % atoms), device_id_type=MESH
        )
    pl.semaphore_wait(barrier, atoms - 1)

    def remote(src, dst, send, recv, device):
        return pltpu.make_async_remote_copy(
            src_ref=src, dst_ref=dst, send_sem=send, recv_sem=recv,
            device_id=device, device_id_type=MESH,
        )

    def spot(atom):
        return orbitals.at[pl.ds(atom * per, per)]

    def to_partner(k, atom, src):
        return remote(src, spot(atom), sx.at[k], rh.at[atom], at_atom(hi * 2 + 1 - lo))

    def along(atom, src, sem, step):
        return remote(src, spot(atom), sem, rh.at[atom], at_atom(me + 2 * step))

    left_ok, right_ok = hi > 0, hi < planes - 1

    @pl.when(left_ok)
    def _():
        along(me, own_ref, sz0.at[0], -1).start()

    @pl.when(right_ok)
    def _():
        along(me, own_ref, sz0.at[1], 1).start()

    to_partner(0, me, own_ref).start()
    own = pltpu.make_async_copy(own_ref, spot(me), local_sem.at[0])
    own.start()

    def plane_of(k):
        half = (k + 1) // 2
        return hi + half * (1 - 2 * (k % 2))

    def valid(k):
        p = plane_of(k)
        return (p >= 0) & (p < planes)

    def forward_ok(k):
        target = hi - (1 - 2 * (k % 2))
        return valid(k) & (target >= 0) & (target < planes)

    def wait_block(atom):
        remote(own_ref, spot(atom), sx.at[0], rh.at[atom], at_atom(hi * 2 + 1 - lo)).wait_recv()

    @pl.loop(1, 2 * planes - 1)
    def _(k):
        @pl.when(valid(k))
        def _():
            atom = plane_of(k) * 2 + lo
            wait_block(atom)

            @pl.when(forward_ok(k))
            def _():
                along(atom, spot(atom), sz.at[k], -(1 - 2 * (k % 2))).start()

            to_partner(k, atom, spot(atom)).start()

    @pl.loop(0, planes)
    def _(p):
        wait_block(p * 2 + 1 - lo)

    own.wait()

    def half_block(place, part):
        slot, nu = order_ref[place], nu_ref[place]
        right = orbitals[nu]
        left = three_ref[slot, part * share:(part + 1) * share] * mask_ref[slot][None, :, :]
        value = jnp.dot(
            left.reshape(share * size, size), right, preferred_element_type=jnp.float32
        )
        return value.reshape(share, size, occ).astype(jnp.bfloat16)

    def target_of(j):
        return (pos + j % (middle - 1) + 1) % middle

    def block(part, j, lane, device):
        return remote(
            outgoing.at[part, j], arrived.at[part, lane], sd.at[part, j], rd.at[part, lane], device
        )

    def start_sends(first, owner_side, part):
        @pl.loop(first, first + middle - 1)
        def _(j):
            q = target_of(j)
            owner = owner_side * middle + q
            lane = (first // (middle - 1)) * middle + pos

            @pl.loop(0, cap)
            def _(r):
                outgoing[part, j, r] = half_block(owner * cap + r, part)

            device = at_atom(side * middle + q)
            if part == 0:
                remote(code_ref.at[owner], codes.at[lane], sk.at[j], rk.at[lane], device).start()
            block(part, j, lane, device).start()

    def fill_own(lane, owner, sem):
        @pl.loop(0, cap)
        def _(r):
            for part in range(2):
                arrived[part, lane, r] = half_block(owner * cap + r, part)

        keep = pltpu.make_async_copy(code_ref.at[owner], codes.at[lane], sem)
        keep.start()
        keep.wait()

    start_sends(0, 1 - side, 0)
    start_sends(0, 1 - side, 1)
    fill_own(pos, (1 - side) * middle + pos, local_sem.at[1])
    start_sends(middle - 1, side, 0)
    start_sends(middle - 1, side, 1)
    fill_own(middle + pos, me, local_sem.at[2])

    def take(src, part):
        hits = [
            [codes[src, r, b] for r in range(cap)]
            for b in range(per)
        ]

        @pl.loop(0, share * (size // 64))
        def _(n):
            p, row = n // (size // 64), n % (size // 64)
            at = pl.ds(pl.multiple_of(row * 64, 64), 64)
            values = [
                arrived[part, src, r, p, at, :].astype(jnp.float32).reshape(8, 8, occ)
                for r in range(cap)
            ]
            for b in range(per):
                to = pl.ds(pl.multiple_of(b * size + row * 64, 64), 64)
                total = acc[part * share + p, to, :].reshape(8, 8, occ)
                for r in range(cap):
                    total = total + values[r] * hits[b][r][None]
                acc[part * share + p, to, :] = total.reshape(64, occ)

    def take_all(base, part):
        span = pl.ds(part * share, share)
        acc[span] = jnp.zeros((share,) + acc.shape[1:], jnp.float32)
        take(base + pos, part)

        @pl.loop(1, middle)
        def _(i):
            src = (pos + middle - i) % middle
            lane = base + src
            device = at_atom(side * middle + src)
            if part == 0:
                remote(code_ref.at[0], codes.at[lane], sk.at[0], rk.at[lane], device).wait_recv()
            block(part, 0, lane, device).wait_recv()
            take(lane, part)

    across = at_atom((1 - side) * middle + pos)
    crossings = []
    for part in range(2):
        take_all(0, part)
        span = pl.ds(part * share, share)
        summed[span] = acc[span].astype(jnp.bfloat16)
        cross = remote(
            summed.at[span], landed.at[span], cross_sem.at[part], cross_sem.at[2 + part], across
        )
        cross.start()
        crossings.append(cross)
    take_all(middle, 0)
    take_all(middle, 1)
    for part in range(2):
        crossings[part].wait_recv()
        span = pl.ds(part * share, share)
        out_ref[span] = (acc[span] + landed[span].astype(jnp.float32)).astype(jnp.bfloat16)
    for cross in crossings:
        cross.wait_send()

    @pl.when(left_ok)
    def _():
        along(me, own_ref, sz0.at[0], -1).wait_send()

    @pl.when(right_ok)
    def _():
        along(me, own_ref, sz0.at[1], 1).wait_send()

    to_partner(0, me, own_ref).wait_send()

    @pl.loop(1, 2 * planes - 1)
    def _(k):
        @pl.when(valid(k))
        def _():
            to_partner(k, me, own_ref).wait_send()

            @pl.when(forward_ok(k))
            def _():
                along(me, own_ref, sz.at[k], -(1 - 2 * (k % 2))).wait_send()

    @pl.loop(0, 2 * middle - 2)
    def _(j):
        device = at_atom(side * middle + target_of(j))
        block(0, j, 0, device).wait_send()
        block(1, j, 0, device).wait_send()
        remote(code_ref.at[0], codes.at[0], sk.at[j], rk.at[0], device).wait_send()


def route_call(order, nu, three_index, mask, codes, coefficients):
    aux_here, size = three_index.shape[1], three_index.shape[2]
    rows, occ = coefficients.shape
    per = rows // size
    atoms = lax.axis_size("atom")
    planes = atoms // 2
    dma = pltpu.SemaphoreType.DMA
    smem = pl.BlockSpec(memory_space=pltpu.SMEM)
    vmem = pl.BlockSpec(memory_space=pltpu.VMEM)
    return pl.pallas_call(
        functools.partial(route_kernel, atoms),
        out_shape=jax.ShapeDtypeStruct((aux_here, rows, occ), jnp.bfloat16),
        in_specs=[smem, smem, vmem, vmem, vmem, vmem],
        out_specs=vmem,
        scratch_shapes=[
            pltpu.VMEM((atoms * per, size, occ), jnp.bfloat16),
            pltpu.VMEM((2, atoms - 2, CAP, aux_here // 2, size, occ), jnp.bfloat16),
            pltpu.VMEM((2, atoms, CAP, aux_here // 2, size, occ), jnp.bfloat16),
            pltpu.VMEM((atoms, CAP, per, 8, 128), jnp.float32),
            pltpu.VMEM((aux_here, rows, occ), jnp.float32),
            pltpu.VMEM((aux_here, rows, occ), jnp.bfloat16),
            pltpu.VMEM((aux_here, rows, occ), jnp.bfloat16),
            dma((3,)),
            dma((2 * planes - 1,)),
            dma((2,)),
            dma((2 * planes - 1,)),
            dma((atoms,)),
            dma((2, atoms - 2)),
            dma((2, atoms)),
            dma((atoms - 2,)),
            dma((atoms,)),
            dma((4,)),
        ],
        compiler_params=pltpu.CompilerParams(
            collective_id=1, has_side_effects=True, vmem_limit_bytes=60 * 1024 * 1024
        ),
    )(order, nu, three_index, mask, codes, coefficients.reshape(per, size, occ))


def fused_kernel(
    planes, auxes, split,
    owner_ref, sub_ref, nu_ref, live_ref, three_hbm, mask_ref, coef_ref, fit_ref, out_ref,
    kron_ref, three, mexp, mrows, orb, order, nus, hits, hits_in, keep, xs, xr, up, dn, zb, own_rows, rows_all, fitted, kron, cs, cr,
    local_sem, orb_recv, orb_own, orb_line, orb_x, orb_core, code_sem, kron_send, kron_recv,
    x_send, x_recv, up_send, up_recv, dn_send, dn_recv,
    own_sem, line_up, line_dn, line_recv, b_send, b_recv, a_send, a_recv, c_send, c_recv,
):
    slot_count, aux_here, size, _ = three_hbm.shape
    per = coef_ref.shape[0]
    rows, occ = per * size, coef_ref.shape[2]
    atoms = planes * 2
    half = per // 2
    chunks, part = aux_here * split, size // split
    group = per * part
    shells = mask_ref.shape[1]
    shell = size // shells
    me = lax.axis_index("atom")
    ax = lax.axis_index("aux")
    z, x = me // 2, me % 2
    y, c = ax // 2, ax % 2
    ys = auxes // 2
    above, below = {"atom": me + 2, "aux": ax}, {"atom": me - 2, "aux": ax}
    partner = {"atom": z * 2 + 1 - x, "aux": ax}
    core = {"atom": me, "aux": y * 2 + 1 - c}
    has_up, has_dn = z < planes - 1, z > 0

    def at_aux(u):
        return {"atom": me, "aux": u}

    barrier = pltpu.get_barrier_semaphore()

    def greet(device):
        pl.semaphore_signal(barrier, inc=1, device_id=device, device_id_type=MESH)

    greet(partner)
    for d in range(1, auxes):
        greet(at_aux((ax + d) % auxes))

    @pl.when(has_up)
    def _():
        greet(above)

    @pl.when(has_dn)
    def _():
        greet(below)

    load_three = pltpu.make_async_copy(three_hbm, three, local_sem.at[0])
    load_three.start()
    load_orb = pltpu.make_async_copy(coef_ref, orb.at[pl.ds(me * per, per)], local_sem.at[2])
    load_orb.start()

    pl.semaphore_wait(
        barrier, auxes + jnp.minimum(z, 1) + jnp.minimum(planes - 1 - z, 1)
    )

    def remote(src, dst, send, recv, device):
        return pltpu.make_async_remote_copy(
            src_ref=src, dst_ref=dst, send_sem=send, recv_sem=recv,
            device_id=device, device_id_type=MESH,
        )

    def spot(atom, part):
        return orb.at[pl.ds(atom * per + part * half, half)]

    own_part = coef_ref.at[pl.ds(c * half, half)]

    def orb_copy(src, atom, part, send, device):
        return remote(src, spot(atom, part), send, orb_recv.at[atom * 2 + part], device)

    @pl.when(has_up)
    def _():
        orb_copy(own_part, me, c, orb_own.at[0], above).start()

    @pl.when(has_dn)
    def _():
        orb_copy(own_part, me, c, orb_own.at[1], below).start()

    orb_copy(own_part, me, c, orb_own.at[2], partner).start()

    def wait_orb(atom, part):
        orb_copy(own_part, atom, part, orb_own.at[0], partner).wait_recv()

    lane_row = lax.broadcasted_iota(jnp.int32, (8, 128), 0)
    live = live_ref[0]

    @pl.loop(0, atoms)
    def _(o):
        def scan(s, carry):
            count, slots, nu, codes = carry
            hit = owner_ref[s] == o
            code = jnp.where(s < live, sub_ref[s] + 1, 0)
            new = []
            for r in range(CAP):
                take = hit & (count == r)
                new.append((
                    jnp.where(take, s, slots[r]),
                    jnp.where(take, nu_ref[s], nu[r]),
                    jnp.where(take, code, codes[r]),
                ))
            count = count + jnp.where(hit, 1, 0)
            return count, tuple(v[0] for v in new), tuple(v[1] for v in new), tuple(v[2] for v in new)

        zero = jnp.int32(0)
        zeros = (zero,) * CAP
        _, slots, nu, codes = lax.fori_loop(0, slot_count, scan, (zero, zeros, zeros, zeros))
        for r in range(CAP):
            index = ((o % 2) * planes + o // 2) * CAP + r
            order[index] = slots[r]
            nus[index] = nu[r]
            hits[index] = jnp.where(lane_row == codes[r] - 1, 1.0, 0.0)

    code_count = planes * CAP
    send_codes = remote(
        hits.at[pl.ds((1 - x) * code_count, code_count)], hits_in, code_sem.at[0], code_sem.at[1], partner
    )
    send_codes.start()

    def iota(shape, dim):
        return lax.broadcasted_iota(jnp.int32, shape, dim)

    aux_total = auxes * aux_here
    strip = kron_ref.shape[0] // aux_here
    tall, wide = kron_ref.shape
    down = jnp.where(iota((tall, aux_here), 0) // strip == iota((tall, aux_here), 1), 1.0, 0.0)
    along = jnp.where(iota((aux_total, wide), 1) // strip == iota((aux_total, wide), 0), 1.0, 0.0)
    spread_rows = jnp.dot(down, fit_ref[...].astype(jnp.float32), preferred_element_type=jnp.float32)
    spread_all = jnp.dot(spread_rows, along, preferred_element_type=jnp.float32)
    same = iota((tall, wide), 0) % strip == iota((tall, wide), 1) % strip
    kron_ref[...] = jnp.where(same, spread_all, 0.0).astype(jnp.bfloat16)
    load_kron = pltpu.make_async_copy(
        kron_ref, kron.at[pl.ds(pl.multiple_of(ax * kron_ref.shape[0], kron_ref.shape[0]), kron_ref.shape[0])], local_sem.at[1]
    )
    load_kron.start()

    spread = jnp.where(
        lax.broadcasted_iota(jnp.int32, (shells, size), 1) // shell
        == lax.broadcasted_iota(jnp.int32, (shells, size), 0), 1.0, 0.0
    )
    for m in range(shells):
        mrows[m] = lax.dot_general(
            mask_ref[m].astype(jnp.float32), spread, (((0,), (0,)), ((), ())),
            preferred_element_type=jnp.float32,
        )

    @pl.loop(0, slot_count)
    def _(s):
        for m in range(shells):
            mexp[s, m * shell:(m + 1) * shell, :] = jnp.broadcast_to(
                mrows[m, pl.ds(s, 1), :], (shell, size)
            ).astype(jnp.bfloat16)

    def pass_orb(p, upward):
        atom = p * 2 + x
        wait_orb(atom, c)
        if upward:
            @pl.when(has_up)
            def _():
                orb_copy(spot(atom, c), atom, c, orb_line.at[p], above).start()
        else:
            @pl.when(has_dn)
            def _():
                orb_copy(spot(atom, c), atom, c, orb_line.at[p], below).start()
        orb_copy(spot(atom, c), atom, c, orb_x.at[p], partner).start()
        orb_copy(spot(atom, c), atom, c, orb_core.at[atom], core).start()

    def hand_orb(p):
        atom = p * 2 + 1 - x
        wait_orb(atom, c)
        orb_copy(spot(atom, c), atom, c, orb_core.at[atom], core).start()

    @pl.loop(1, planes)
    def _(d):
        @pl.when(z - d >= 0)
        def _():
            pass_orb(z - d, True)

        @pl.when(z + d < planes)
        def _():
            pass_orb(z + d, False)

    hand_orb(z)

    @pl.loop(1, planes)
    def _(d):
        @pl.when(z - d >= 0)
        def _():
            hand_orb(z - d)

        @pl.when(z + d < planes)
        def _():
            hand_orb(z + d)

    load_kron.wait()
    load_orb.wait()

    def kron_part(u):
        return kron.at[pl.ds(pl.multiple_of(u * kron_ref.shape[0], kron_ref.shape[0]), kron_ref.shape[0])]

    for d in range(1, auxes):
        remote(kron_ref, kron_part(ax), kron_send.at[d], kron_recv.at[ax], at_aux((ax + d) % auxes)).start()

    @pl.loop(0, planes)
    def _(p):
        wait_orb(p * 2 + 1 - x, 1 - c)

        @pl.when(p != z)
        def _():
            wait_orb(p * 2 + x, 1 - c)

    load_three.wait()
    send_codes.wait_recv()

    def half_block(index, k):
        slot, nu = order[index], nus[index]
        at = pl.ds(pl.multiple_of((k % split) * part, part), part)
        left = three[slot, k // split, at, :] * mexp[slot, at, :]
        return jnp.dot(left, orb[nu], preferred_element_type=jnp.float32).astype(jnp.bfloat16)

    def x_copy(k):
        return remote(xs.at[k], xr.at[k], x_send.at[k], x_recv.at[k], partner)

    def add_dense(p, k, extras, target):
        own_hits = [
            [jnp.broadcast_to(hits[(x * planes + p) * CAP + r, b:b + 1, :], (8, 128))[None] for r in range(CAP)]
            for b in range(per)
        ]
        in_hits = [
            [jnp.broadcast_to(hits_in[p * CAP + r, b:b + 1, :], (8, 128))[None] for r in range(CAP)]
            for b in range(per)
        ]
        shape = (part // 8, 8, occ)
        own = [keep[k, p, r].astype(jnp.float32).reshape(shape) for r in range(CAP)]
        other = [xr[k, p, r].astype(jnp.float32).reshape(shape) for r in range(CAP)]
        for b in range(per):
            to = slice(b * part, (b + 1) * part)
            total = own[0] * own_hits[b][0] + other[0] * in_hits[b][0]
            for r in range(1, CAP):
                total = total + own[r] * own_hits[b][r] + other[r] * in_hits[b][r]
            for extra in extras:
                total = total + extra[p, k, to, :].astype(jnp.float32).reshape(shape)
            value = total.reshape(part, occ).astype(jnp.bfloat16)
            if target is own_rows:
                target[k, to, :] = value
            else:
                target[p, k, to, :] = value

    def up_copy(p, k):
        ref = up.at[p, k]
        return remote(ref, ref, up_send.at[p, k], up_recv.at[p, k], above)

    def dn_copy(p, k):
        ref = dn.at[p, k]
        return remote(ref, ref, dn_send.at[p, k], dn_recv.at[p, k], below)

    def lane_of(p):
        return (p + 2 * planes - ax - 1) % planes

    def b_lane(sender, target):
        return planes - 1 + (sender + auxes - target) % auxes

    def line_copy(src, p, k, send, device):
        return remote(src, zb.at[lane_of(p), k], send, line_recv.at[p, k], device)

    def b_copy(src, p, k):
        return remote(src, zb.at[b_lane(ax, p), k], b_send.at[p, k], b_recv.at[ax, k], at_aux(p))

    def a_piece(column, u, k):
        return rows_all.at[column, u, k]

    def a_copy(column, u, k, which, device):
        ref = a_piece(column, u, k)
        return remote(ref, ref, a_send.at[which, k], a_recv.at[column, u, k], device)

    def own_a_copy(k, which, device):
        return remote(
            own_rows.at[k], a_piece(x, ax, k), a_send.at[which, k], a_recv.at[x, ax, k], device
        )

    def own_copy(k):
        return pltpu.make_async_copy(own_rows.at[k], a_piece(x, ax, k), own_sem.at[k])

    def y_devices():
        return [((y + d) % ys) * 2 + c for d in range(1, ys)]

    def inside(k):
        return (k >= 0) & (k < chunks)

    def reduce_rows(t, zz):
        if zz < planes - 1:
            ku = t - 1 - zz

            @pl.when(inside(ku))
            def _():
                for p in range(planes - 1, zz, -1):
                    if zz > 0:
                        up_copy(p, ku).wait_recv()
                    add_dense(p, ku, [up] if zz > 0 else [], up)
                    up_copy(p, ku).start()

        if zz > 0:
            kd = t - planes + zz

            @pl.when(inside(kd))
            def _():
                for p in range(zz):
                    if zz < planes - 1:
                        dn_copy(p, kd).wait_recv()
                    add_dense(p, kd, [dn] if zz < planes - 1 else [], dn)
                    dn_copy(p, kd).start()

        kh = t - 1 - max(zz, planes - 1 - zz)

        @pl.when(inside(kh))
        def _():
            extras = []
            if zz > 0:
                up_copy(zz, kh).wait_recv()
                extras.append(up)
            if zz < planes - 1:
                dn_copy(zz, kh).wait_recv()
                extras.append(dn)
            add_dense(zz, kh, extras, own_rows)
            mine = own_rows.at[kh]
            own_copy(kh).start()
            if zz < planes - 1:
                line_copy(mine, zz, kh, line_up.at[zz, kh], above).start()
            if zz > 0:
                line_copy(mine, zz, kh, line_dn.at[zz, kh], below).start()
            own_a_copy(kh, 0, partner).start()
            for n, u in enumerate(y_devices()):
                own_a_copy(kh, 7 + 2 * n, at_aux(u)).start()
            own_a_copy(kh, 1, core).start()

    def pass_line(t, zz, p):
        kz = t - 1 - max(p, planes - 1 - p) - abs(zz - p)

        @pl.when(inside(kz))
        def _():
            piece = zb.at[lane_of(p), kz]
            line_copy(piece, p, kz, line_up.at[p, kz], above).wait_recv()
            if p < zz < planes - 1:
                line_copy(piece, p, kz, line_up.at[p, kz], above).start()
            if p > zz > 0:
                line_copy(piece, p, kz, line_dn.at[p, kz], below).start()

            @pl.when(p != ax)
            def _():
                b_copy(piece, p, kz).start()

    def pass_rows(t, zz):
        ka = t - 2 - max(zz, planes - 1 - zz)

        @pl.when(inside(ka))
        def _():
            a_copy(1 - x, ax, ka, 0, partner).wait_recv()
            for n, u in enumerate(y_devices()):
                a_copy(1 - x, ax, ka, 8 + 2 * n, at_aux(u)).start()
            a_copy(1 - x, ax, ka, 2, core).start()
            for n, u in enumerate(y_devices()):
                a_copy(x, u, ka, 0, partner).wait_recv()
                a_copy(x, u, ka, 7 + 2 * (ys - 1) + 2 * n, core).start()

        kb = t - 3 - max(zz, planes - 1 - zz)

        @pl.when(inside(kb))
        def _():
            for n, u in enumerate(y_devices()):
                a_copy(1 - x, u, kb, 0, partner).wait_recv()
                a_copy(1 - x, u, kb, 8 + 2 * (ys - 1) + 2 * n, core).start()

        for d in range(1, planes):
            for p in (zz - d, zz + d):
                if 0 <= p < planes:
                    pass_line(t, zz, p)

    @pl.loop(0, chunks + 2 * planes - 1)
    def _(t):
        @pl.when(t < chunks)
        def _():
            @pl.loop(0, planes)
            def _(p):
                for r in range(CAP):
                    xs[t, p, r] = half_block(((1 - x) * planes + p) * CAP + r, t)

            x_copy(t).start()

            @pl.loop(0, planes)
            def _(p):
                for r in range(CAP):
                    keep[t, p, r] = half_block((x * planes + p) * CAP + r, t)

        @pl.when((t >= 1) & (t <= chunks))
        def _():
            x_copy(t - 1).wait_recv()

        for zz in range(planes):
            @pl.when(z == zz)
            def _():
                reduce_rows(t, zz)
                pass_rows(t, zz)

    for d in range(1, auxes):
        remote(kron_ref, kron_part((ax + d) % auxes), kron_send.at[d], kron_recv.at[(ax + d) % auxes], core).wait_recv()

    @pl.loop(0, chunks)
    def _(k):
        own_copy(k).wait()
        for d in range(ys):
            u = ((y + d) % ys) * 2 + 1 - c
            for column in range(2):
                a_copy(column, u, k, 0, partner).wait_recv()

        @pl.when(z != ax)
        def _():
            for d in range(1, auxes):
                u = (ax + d) % auxes
                remote(
                    zb.at[b_lane(u, ax), k], zb.at[b_lane(u, ax), k],
                    b_send.at[0, k], b_recv.at[u, k], core,
                ).wait_recv()

    total_aux = auxes * aux_here
    pairs = [(u, p) for u in range(auxes) for p in range(aux_here)]

    halves = 2
    turns = group // (2 * strip) // halves

    def mix(load, v):
        for h in range(split):
            @pl.loop(v * turns, (v + 1) * turns)
            def _(j):
                right = jnp.concatenate([
                    jnp.concatenate([
                        load(u, p * split + h, pl.ds(pl.multiple_of((2 * j + e) * strip, strip), strip))
                        for u, p in pairs
                    ], axis=0)
                    for e in range(2)
                ], axis=-1)
                value = jnp.dot(kron[...], right, preferred_element_type=jnp.float32).astype(jnp.bfloat16)
                for e in range(2):
                    place = (2 * j + e) * strip
                    to = (place // part) * size + h * part + place % part
                    to = pl.ds(pl.multiple_of(to, strip), strip)
                    for q in range(total_aux):
                        fitted[to, q * occ:(q + 1) * occ] = value[
                            q * strip:(q + 1) * strip, e * occ:(e + 1) * occ
                        ]

    def mix_half(v):
        @pl.when(z == ax)
        def _():
            mix(lambda u, k, at: rows_all[x, u, k, at, :], v)

        @pl.when(z != ax)
        def _():
            mix(lambda u, k, at: zb[b_lane(u, ax), k, at, :], v)

    width = rows // halves

    def product(column, h, v):
        left = jnp.concatenate([rows_all[column, u, p * split + h] for u, p in pairs], axis=-1)
        return lax.dot_general(
            left, fitted[v * width:(v + 1) * width, :], (((1,), (1,)), ((), ())),
            preferred_element_type=jnp.float32,
        )

    def c_copy(h, v):
        return remote(cs.at[v, h], cr.at[v, h], c_send.at[v, h], c_recv.at[v, h], partner)

    def place_rows(h, v, column, value):
        for b in range(per):
            to = pl.ds(pl.multiple_of(b * size + h * part, part), part)
            cols = pl.ds(pl.multiple_of(column * rows + v * width, width), width)
            out_ref[to, cols] = value[b * part:(b + 1) * part, :]

    for v in range(halves):
        mix_half(v)

        @pl.loop(0, split)
        def _(h):
            cs[v, h] = product(1 - x, h, v).astype(jnp.bfloat16)
            c_copy(h, v).start()

    for v in range(halves):
        @pl.loop(0, split)
        def _(h):
            place_rows(h, v, x, product(x, h, v))

    for v in range(halves):
        @pl.loop(0, split)
        def _(h):
            c_copy(h, v).wait_recv()
            place_rows(h, v, 1 - x, cr[v, h].astype(jnp.float32))

    @pl.when(has_up)
    def _():
        orb_copy(own_part, me, c, orb_own.at[0], above).wait_send()

    @pl.when(has_dn)
    def _():
        orb_copy(own_part, me, c, orb_own.at[1], below).wait_send()

    orb_copy(own_part, me, c, orb_own.at[2], partner).wait_send()
    send_codes.wait_send()

    @pl.loop(0, planes)
    def _(p):
        @pl.when(p != z)
        def _():
            @pl.when(((p < z) & has_up) | ((p > z) & has_dn))
            def _():
                orb_copy(own_part, me, c, orb_line.at[p], partner).wait_send()

            orb_copy(own_part, me, c, orb_x.at[p], partner).wait_send()
            orb_copy(own_part, me, c, orb_core.at[p * 2 + x], partner).wait_send()

        orb_copy(own_part, me, c, orb_core.at[p * 2 + 1 - x], partner).wait_send()

    for d in range(1, auxes):
        remote(kron_ref, kron_part(ax), kron_send.at[d], kron_recv.at[ax], core).wait_send()

    @pl.loop(0, chunks)
    def _(k):
        x_copy(k).wait_send()
        for which in range(7 + 4 * (ys - 1)):
            if which < 3 or which >= 7:
                a_copy(x, ax, k, which, partner).wait_send()

        @pl.loop(0, planes)
        def _(p):
            @pl.when(p > z)
            def _():
                up_copy(p, k).wait_send()

            @pl.when(p < z)
            def _():
                dn_copy(p, k).wait_send()

            @pl.when((p <= z) & has_up)
            def _():
                line_copy(a_piece(x, ax, k), z, k, line_up.at[p, k], partner).wait_send()

            @pl.when((p >= z) & has_dn)
            def _():
                line_copy(a_piece(x, ax, k), z, k, line_dn.at[p, k], partner).wait_send()

            @pl.when((p != z) & (p != ax))
            def _():
                b_copy(a_piece(x, ax, k), p, k).wait_send()

    @pl.loop(0, split)
    def _(h):
        for v in range(halves):
            c_copy(h, v).wait_send()


def fused_scratch(planes, auxes, split, slot_count, aux_here, size, occ, per, shells, kron_rows):
    atoms, rows, chunks, ys = planes * 2, per * size, aux_here * split, auxes // 2
    part, group = size // split, rows // split
    dma = pltpu.SemaphoreType.DMA
    half = jnp.bfloat16
    ways = 7 + 4 * (ys - 1)
    buffers = [
        pltpu.VMEM((kron_rows, auxes * kron_rows), half),
        pltpu.VMEM((slot_count, aux_here, size, size), half),
        pltpu.VMEM((slot_count, size, size), half),
        pltpu.VMEM((shells, slot_count, size), jnp.float32),
        pltpu.VMEM((atoms * per, size, occ), half),
        pltpu.SMEM((atoms * CAP,), jnp.int32),
        pltpu.SMEM((atoms * CAP,), jnp.int32),
        pltpu.VMEM((atoms * CAP, 8, 128), jnp.float32),
        pltpu.VMEM((planes * CAP, 8, 128), jnp.float32),
        pltpu.VMEM((chunks, planes, CAP, part, occ), half),
        pltpu.VMEM((chunks, planes, CAP, part, occ), half),
        pltpu.VMEM((chunks, planes, CAP, part, occ), half),
        pltpu.VMEM((planes, chunks, group, occ), half),
        pltpu.VMEM((planes, chunks, group, occ), half),
        pltpu.VMEM((planes + auxes - 1, chunks, group, occ), half),
        pltpu.VMEM((chunks, group, occ), half),
        pltpu.VMEM((2, auxes, chunks, group, occ), half),
        pltpu.VMEM((rows, auxes * aux_here * occ), half),
        pltpu.VMEM((auxes * kron_rows, auxes * kron_rows), half),
        pltpu.VMEM((2, split, group, rows // 2), half),
        pltpu.VMEM((2, split, group, rows // 2), half),
    ]
    semaphores = [
        dma((3,)),
        dma((atoms * 2,)),
        dma((3,)),
        dma((planes,)),
        dma((planes,)),
        dma((atoms,)),
        dma((2,)),
        dma((auxes,)),
        dma((auxes,)),
        dma((chunks,)),
        dma((chunks,)),
        dma((planes, chunks)),
        dma((planes, chunks)),
        dma((planes, chunks)),
        dma((planes, chunks)),
        dma((chunks,)),
        dma((planes, chunks)),
        dma((planes, chunks)),
        dma((planes, chunks)),
        dma((planes, chunks)),
        dma((auxes, chunks)),
        dma((ways, chunks)),
        dma((2, auxes, chunks)),
        dma((2, split)),
        dma((2, split)),
    ]
    return buffers, semaphores


VMEM_LIMIT = 60 * 1024 * 1024
STRIP = 16
SPLIT = 2


def fused_plan(planes, auxes, three_index, pair_mask, coefficients):
    slot_count, aux_here, size, _ = three_index.shape
    rows, occ = coefficients.shape
    per, shells = rows // size, pair_mask.shape[1]
    if planes != auxes or per % 2 or per > 8 or size % (32 * SPLIT) or shells % 8 or rows % (2 * 128):
        return None
    buffers, semaphores = fused_scratch(
        planes, auxes, SPLIT, slot_count, aux_here, size, occ, per, shells, aux_here * STRIP
    )
    held = rows * 2 * rows * 4 + 2 * rows * occ * 2
    for ref in buffers:
        held += math.prod(ref.shape) * jnp.dtype(ref.dtype).itemsize
    if held > VMEM_LIMIT - 4 * 1024 * 1024:
        return None
    return buffers + semaphores


def fused_call(plan, planes, auxes, three_index, pair_mask, owners, subs, nus, live, coefficients, fit_rows):
    slot_count, aux_here, size, _ = three_index.shape
    rows, occ = coefficients.shape
    shells = pair_mask.shape[1]
    smem = pl.BlockSpec(memory_space=pltpu.SMEM)
    vmem = pl.BlockSpec(memory_space=pltpu.VMEM)
    return pl.pallas_call(
        functools.partial(fused_kernel, planes, auxes, SPLIT),
        out_shape=jax.ShapeDtypeStruct((rows, 2 * rows), jnp.float32),
        in_specs=[smem] * 4 + [pl.BlockSpec(memory_space=pl.ANY)] + [vmem] * 3,
        out_specs=vmem,
        scratch_shapes=plan,
        compiler_params=pltpu.CompilerParams(
            collective_id=2, has_side_effects=True, vmem_limit_bytes=VMEM_LIMIT
        ),
    )(
        owners, subs, nus, live, three_index, pair_mask.transpose(1, 2, 0),
        coefficients.reshape(rows // size, size, occ), fit_rows,
    )


def per_device(
    three_index, pair_mask, pair_owner, pair_sub, pair_nu, live_count, coefficients, fit_matrix
):
    slot_count, aux_here, block_size, _ = three_index.shape
    rows_here, occupied = coefficients.shape
    atom_count = lax.axis_size("atom")
    aux_total = fit_matrix.shape[1]
    planes, auxes = atom_count // 2, lax.axis_size("aux")
    plan = fused_plan(planes, auxes, three_index, pair_mask, coefficients)
    if plan is not None:
        total = fused_call(
            plan, planes, auxes, three_index, pair_mask, pair_owner[:, 0], pair_sub, pair_nu,
            live_count, coefficients, fit_matrix,
        )
        return total * (aux_total * occupied) ** (-0.5)
    shell_size = block_size // pair_mask.shape[1]
    expanded = jnp.repeat(jnp.repeat(pair_mask, shell_size, 1), shell_size, 2).astype(jnp.bfloat16)
    owners = pair_owner[:, 0]
    ahead = jnp.arange(slot_count)[None, :] < jnp.arange(slot_count)[:, None]
    rank_within = jnp.sum(((owners[:, None] == owners[None, :]) & ahead).astype(jnp.int32), 1)
    placement = owners * CAP + rank_within
    routing = (jnp.arange(atom_count * CAP)[:, None] == placement[None, :]).astype(jnp.int32)
    slots = jnp.arange(slot_count, dtype=jnp.int32)

    def placed(values):
        return jnp.sum(routing * values[None, :], 1)

    live_codes = placed(jnp.where(slots < live_count[0], pair_sub + 1, 0))
    blocks = jnp.arange(rows_here // block_size)
    hits = (live_codes[:, None] == blocks[None, :] + 1).astype(jnp.float32)
    hits = hits.reshape(atom_count, CAP, blocks.shape[0], 1, 1)
    local_rows = route_call(
        placed(slots),
        placed(pair_nu),
        three_index,
        expanded,
        jnp.broadcast_to(hits, hits.shape[:3] + (8, 128)),
        coefficients,
    )
    total = exchange_call(local_rows, fit_matrix.astype(jnp.float32))
    return total * (aux_total * occupied) ** (-0.5)


def solution(mesh):
    in_specs = (
        P("atom", "aux", None, None),
        P("atom", None, None),
        P("atom", None),
        P("atom"),
        P("atom"),
        P("atom"),
        P("atom", None),
        P("aux", None),
    )
    out_specs = P("atom", "aux")
    return jax.shard_map(
        per_device, mesh=mesh, in_specs=in_specs, out_specs=out_specs, check_vma=False
    )
```
